256 devices in a mesh: tunnel: 32 (over z_hi, x, core), group: 8 (over z_lo, y).
Axes of the slice: x: 4, y: 4, z: 8 (z_hi: 4, z_lo: 2; z = z_hi * 2 + z_lo), core: 2. Of those that a mesh axis runs over, the one named last changes fastest.
Arguments:
- velocity: float32 [3, 512, 512, 256], P(None, ('tunnel', 'group')), may hold values from -6 to 6
- obstacle: int32 [512, 512, 256], P(('tunnel', 'group')), may hold values 0 or 1
- pressure: float32 [512, 512, 256], P('tunnel', 'group'), may hold values from -6 to 6
Outputs:
- corrected: float32 [3, 512, 512, 256], P(None, ('tunnel', 'group'))
- potential: float32 [512, 512, 256], P('tunnel', 'group')
The draws below stay inside these ranges and needn't reach their ends.
All inputs are finite; a program needn't handle non-finite values. No bound on the sum of `obstacle` on one device may be relied on, other than what follows from the above.
Results may differ from the reference program's by a relative error of at most 0.00018.
Values sent between devices are 32-bit elements; how exact they have to be, the bound alone decides.
A program may use at most 256 MiB of HBM per device.

```python
import math
import jax
import jax.numpy as jnp
from jax import lax

NY = 512
NZ = 256
LEVELS = 3
SWEEPS = 2
COARSE_SWEEPS = 4
X = 512


def plant(values, own_key, smallest, high):
    place = [jax.random.randint(jax.random.fold_in(own_key, axis), (), 0, length) for axis, length in enumerate(values.shape)]
    main_axis = values.shape.index(max(values.shape))
    neighbour = place[:main_axis] + [(place[main_axis] + 1) % values.shape[main_axis]] + place[main_axis + 1:]
    return values.at[tuple(place)].set(smallest).at[tuple(neighbour)].set(high)


def block_scale(own_key, dims, split, least, top_value):
    def one(position, shards_of):
        steps = jax.random.uniform(jax.random.fold_in(jax.random.fold_in(own_key, 6), position), (shards_of,), jnp.float32, least / len(split), top_value / len(split))
        return jnp.repeat(jnp.exp(steps), dims[position] // shards_of).reshape((-1,) + (1,) * (len(dims) - position - 1))

    factor_of = one(*split[0])
    for cut in split[1:]:
        factor_of = factor_of * one(*cut)
    return factor_of


def bell_draw(rng, dims, deviation, limit, split=(), kind=jnp.bfloat16):
    entries = deviation * jax.random.normal(rng, dims, jnp.float32)
    if split:
        entries = entries * block_scale(rng, dims, split, -0.22, 0.18)
    return jnp.clip(entries, -limit, limit).astype(kind)


def setup_inputs(seed: int = 0) -> dict:
    streams_of = jax.random.split(jax.random.key(seed), 4)
    return {
        "velocity": bell_draw(streams_of[0], (3, X, NY, NZ), 1.0, 6.0, ((1, 256),), jnp.float32),
        "obstacle": plant((jax.random.randint(streams_of[1], (X, NY, NZ), 0, 8) < 1).astype(jnp.int32), jax.random.fold_in(streams_of[1], 1), 0, 1),
        "pressure": bell_draw(streams_of[2], (X, NY, NZ), 1.0, 6.0, ((0, 32), (1, 8)), jnp.float32),
    }


time_step = 0.1
viscosity = 0.05
relax_weight = 0.8
highest = lax.Precision.HIGHEST


def compact_tables(count):
    indices = jnp.arange(count, dtype=jnp.int32)
    product = (indices[:, None] * indices[None, :]) % count
    angles = product.astype(jnp.float32) * (2.0 * math.pi / count)
    cosines = jnp.cos(angles)
    sines = jnp.sin(angles)
    theta = indices.astype(jnp.float32) * (2.0 * math.pi / count)
    first_wave = (14.0 / 9.0 * jnp.sin(theta) + jnp.sin(2.0 * theta) / 18.0) / (1.0 + 2.0 / 3.0 * jnp.cos(theta))
    second_wave = (24.0 / 11.0 * (1.0 - jnp.cos(theta)) + 3.0 / 22.0 * (1.0 - jnp.cos(2.0 * theta))) / (1.0 + 4.0 / 11.0 * jnp.cos(theta))
    first_matrix = (jnp.dot(cosines * first_wave, sines.T, precision=highest) - jnp.dot(sines * first_wave, cosines.T, precision=highest)) / count
    second_matrix = -(jnp.dot(cosines * second_wave, cosines.T, precision=highest) + jnp.dot(sines * second_wave, sines.T, precision=highest)) / count
    return first_matrix, second_matrix


def along_rows(matrix, field):
    return jnp.einsum('ij,...jz->...iz', matrix, field, precision=highest)


def along_depth(matrix, field):
    return jnp.einsum('...j,ij->...i', field, matrix, precision=highest)


def stream_first(field, axis):
    ahead = jnp.roll(field, -1, axis)
    behind = jnp.roll(field, 1, axis)
    ahead_two = jnp.roll(field, -2, axis)
    behind_two = jnp.roll(field, 2, axis)
    return (8.0 * (ahead - behind) - (ahead_two - behind_two)) / 12.0


def stream_second(field, axis):
    ahead = jnp.roll(field, -1, axis)
    behind = jnp.roll(field, 1, axis)
    ahead_two = jnp.roll(field, -2, axis)
    behind_two = jnp.roll(field, 2, axis)
    return (16.0 * (ahead + behind) - (ahead_two + behind_two) - 30.0 * field) / 12.0


def neighbours(field):
    total = jnp.roll(field, -1, 0) + jnp.roll(field, 1, 0)
    total = total + jnp.roll(field, -1, 1) + jnp.roll(field, 1, 1)
    return total + jnp.roll(field, -1, 2) + jnp.roll(field, 1, 2)


def relax(field, source_term, scale):
    return field + relax_weight / 6.0 * (neighbours(field) - 6.0 * field - scale * source_term)


def restrict(field):
    planes, rows, depth = field.shape
    blocks = field.reshape(planes // 2, 2, rows // 2, 2, depth // 2, 2)
    return jnp.sum(blocks, axis=(1, 3, 5)) * 0.125


def prolong(field):
    return jnp.repeat(jnp.repeat(jnp.repeat(field, 2, 0), 2, 1), 2, 2)


def cycle(field, source_term, level):
    scale = 4.0 ** level
    if level == LEVELS - 1:
        field = jnp.zeros_like(source_term)
        for sweep_index in range(COARSE_SWEEPS):
            field = relax(field, source_term, scale)
        return field
    for sweep_index in range(SWEEPS):
        field = relax(field, source_term, scale)
    leftover = source_term - (neighbours(field) - 6.0 * field) / scale
    coarse_source = restrict(leftover)
    coarse = cycle(jnp.zeros_like(coarse_source), coarse_source, level + 1)
    field = field + prolong(coarse)
    for sweep_index in range(SWEEPS):
        field = relax(field, source_term, scale)
    return field


def reference(velocity, obstacle, pressure):
    rows_first, rows_second = compact_tables(NY)
    depth_first, depth_second = compact_tables(NZ)
    keep = 1.0 - obstacle.astype(jnp.float32)
    advect = velocity[0] * stream_first(velocity, 1)
    advect = advect + velocity[1] * along_rows(rows_first, velocity)
    advect = advect + velocity[2] * along_depth(depth_first, velocity)
    diffusion = stream_second(velocity, 1) + along_rows(rows_second, velocity) + along_depth(depth_second, velocity)
    tendency = -advect + viscosity * diffusion
    star = (velocity + time_step * tendency) * keep
    source = stream_first(star[0], 0) + along_rows(rows_first, star[1]) + along_depth(depth_first, star[2])
    potential = cycle(pressure, source, 0)
    gradient = jnp.stack([stream_first(potential, 0), along_rows(rows_first, potential), along_depth(depth_first, potential)])
    corrected = (star - gradient) * keep
    return corrected, potential
```

```python
import functools
import math

import jax
import jax.numpy as jnp
import numpy as np
from jax import lax
from jax.experimental import pallas as pl
from jax.experimental.pallas import tpu as pltpu
from jax.sharding import PartitionSpec as P

time_step = 0.1
viscosity = 0.05
relax_weight = 0.8
high = lax.Precision.HIGH
highest = lax.Precision.HIGHEST
MESH = pl.DeviceIdType.MESH

ROWS = 8
PLANES_P = 6
PLANES_U = 7
PLANES_S = 5
PLANES_1 = 5
PLANES_2 = 5
WAYS = [(dx, dy) for dx in (-1, 0, 1) for dy in (-1, 0, 1) if (dx, dy) != (0, 0)]


def compact_tables(count):
    indices = np.arange(count)
    angles = (indices[:, None] * indices[None, :] % count) * (2.0 * math.pi / count)
    cosines = np.cos(angles)
    sines = np.sin(angles)
    theta = indices * (2.0 * math.pi / count)
    first_wave = (14.0 / 9.0 * np.sin(theta) + np.sin(2.0 * theta) / 18.0) / (
        1.0 + 2.0 / 3.0 * np.cos(theta)
    )
    second_wave = (
        24.0 / 11.0 * (1.0 - np.cos(theta)) + 3.0 / 22.0 * (1.0 - np.cos(2.0 * theta))
    ) / (1.0 + 4.0 / 11.0 * np.cos(theta))
    first = ((cosines * first_wave) @ sines.T - (sines * first_wave) @ cosines.T) / count
    second = -((cosines * second_wave) @ cosines.T + (sines * second_wave) @ sines.T) / count
    return first.astype(np.float32), second.astype(np.float32)


def along_rows(matrix, field):
    return jnp.einsum("ij,...jz->...iz", matrix, field, precision=high)


def along_depth(matrix, field):
    return jnp.einsum("...j,ij->...i", field, matrix, precision=high)


def shifted(padded, offset, axis):
    count = padded.shape[axis] - 4
    return lax.slice_in_dim(padded, 2 + offset, 2 + offset + count, axis=axis)


def stream_first(padded, axis):
    ahead = shifted(padded, 1, axis) - shifted(padded, -1, axis)
    further = shifted(padded, 2, axis) - shifted(padded, -2, axis)
    return (8.0 * ahead - further) / 12.0


def stream_second(padded, axis):
    ahead = shifted(padded, 1, axis) + shifted(padded, -1, axis)
    further = shifted(padded, 2, axis) + shifted(padded, -2, axis)
    return (16.0 * ahead - further - 30.0 * shifted(padded, 0, axis)) / 12.0


def halo_planes(value, axis):
    size = lax.axis_size(("tunnel", "group"))
    up = [(i, (i + 1) % size) for i in range(size)]
    down = [(j, i) for i, j in up]
    before = lax.ppermute(value, ("tunnel", "group"), up)
    after = lax.ppermute(value, ("tunnel", "group"), down)
    return jnp.concatenate([before, value, after], axis=axis)


def part(step, length, halo):
    if step > 0:
        return length - halo, halo, 0
    if step < 0:
        return 0, halo, halo + length
    return 0, length, halo


def neighbour(sizes, dx, dy):
    me_x = lax.axis_index("tunnel")
    me_y = lax.axis_index("group")
    return (
        lax.rem(me_x + (dx + sizes[0]), sizes[0]),
        lax.rem(me_y + (dy + sizes[1]), sizes[1]),
    )


def enter(sizes):
    barrier = pltpu.get_barrier_semaphore()
    for dx, dy in WAYS:
        pl.semaphore_signal(
            barrier, inc=1, device_id=neighbour(sizes, dx, dy), device_id_type=MESH
        )
    pl.semaphore_wait(barrier, len(WAYS))


def send_tiles(sizes, source, target, shape, planes, sems, origin=(0, 0), lend=0):
    copies = []
    for way, (dx, dy) in enumerate(WAYS):
        from_x, count_x, to_x = part(dx, shape[0], planes)
        from_y, count_y, to_y = part(dy, shape[1], ROWS)
        if dx > 0:
            from_x = shape[0] + lend - planes if lend else from_x
        copies.append(
            pltpu.make_async_remote_copy(
                src_ref=source.at[
                    pl.ds(origin[0] + from_x, count_x), pl.ds(origin[1] + from_y, count_y)
                ],
                dst_ref=target.at[pl.ds(to_x, count_x), pl.ds(to_y, count_y)],
                send_sem=sems[0].at[way],
                recv_sem=sems[1].at[way],
                device_id=neighbour(sizes, dx, dy),
                device_id_type=MESH,
            )
        )
    for copy in copies:
        copy.start()
    return copies


def pressure_kernel(sizes, tile, extended, local_sem, send_sem, recv_sem):
    planes, rows, _ = tile.shape
    own = pltpu.make_async_copy(
        tile, extended.at[pl.ds(PLANES_P, planes), pl.ds(ROWS, rows)], local_sem
    )
    own.start()
    enter(sizes)
    copies = send_tiles(
        sizes, tile, extended, (planes, rows), PLANES_P, (send_sem, recv_sem)
    )
    own.wait()
    for copy in copies:
        copy.wait()


def pressure_halo(pressure, sizes):
    planes, rows, depth = pressure.shape
    return pl.pallas_call(
        functools.partial(pressure_kernel, sizes),
        out_shape=jax.ShapeDtypeStruct(
            (planes + 2 * PLANES_P, rows + 2 * ROWS, depth), jnp.float32
        ),
        in_specs=[pl.BlockSpec(memory_space=pl.ANY)],
        out_specs=pl.BlockSpec(memory_space=pl.ANY),
        scratch_shapes=[
            pltpu.SemaphoreType.DMA,
            pltpu.SemaphoreType.DMA((8,)),
            pltpu.SemaphoreType.DMA((8,)),
        ],
        compiler_params=pltpu.CompilerParams(collective_id=1, has_side_effects=True),
        name="pressure_halo",
    )(pressure)


def around(value):
    rows, depth = value.shape
    total = pltpu.roll(value, 1, 0) + pltpu.roll(value, rows - 1, 0)
    return total + pltpu.roll(value, 1, 1) + pltpu.roll(value, depth - 1, 1)


def sweep(source, target, right, start, stop, offset, scale):
    def body(i, carry):
        mid = source[i]
        total = source[i + 1] + source[i - 1] + around(mid)
        target[i] = mid + (relax_weight / 6.0) * (
            total - 6.0 * mid - scale * right[i + offset]
        )
        return carry

    lax.fori_loop(start, stop, body, 0)


def leftover(source, right, i, offset, scale):
    mid = source[i]
    total = source[i + 1] + source[i - 1] + around(mid)
    return right[i + offset] - (total - 6.0 * mid) * (1.0 / scale)


def exact(a, b):
    return jnp.dot(a, b, precision=highest, preferred_element_type=jnp.float32)


def cycle_kernel(
    sizes,
    fields,
    pressure,
    down_y0,
    down_z0,
    down_y1,
    down_z1,
    up_y1,
    up_z1,
    up_y0,
    up_z0,
    out,
    pa,
    pb,
    src,
    star,
    r1,
    p1a,
    p1b,
    r2s,
    r2,
    c2a,
    c2b,
    local_sem,
    send_sem,
    recv_sem,
):
    _, planes, rows, _ = fields.shape
    planes1, rows1 = planes // 2, rows // 2
    planes2, rows2 = planes // 4, rows // 4
    first_sweep = relax_weight / 6.0

    local = [
        pltpu.make_async_copy(pressure, pa, local_sem.at[0]),
        pltpu.make_async_copy(
            fields.at[0], star.at[pl.ds(PLANES_U, planes), pl.ds(ROWS, rows)], local_sem.at[1]
        ),
        pltpu.make_async_copy(
            fields.at[1], src.at[pl.ds(PLANES_S, planes), pl.ds(ROWS, rows)], local_sem.at[2]
        ),
    ]
    for copy in local:
        copy.start()
    enter(sizes)
    copies = send_tiles(
        sizes, fields.at[0], star, (planes, rows), PLANES_U, (send_sem.at[0], recv_sem.at[0])
    ) + send_tiles(
        sizes, fields.at[1], src, (planes, rows), PLANES_S, (send_sem.at[1], recv_sem.at[1])
    )
    for copy in local + copies:
        copy.wait()

    def divergence(i, carry):
        ahead = star[i + 3] - star[i + 1]
        further = star[i + 4] - star[i]
        src[i] = src[i] + (8.0 * ahead - further) * (1.0 / 12.0)
        return carry

    lax.fori_loop(0, planes + 2 * PLANES_S, divergence, 0)

    sweep(pa, pb, src, 1, planes + 11, -1, 1.0)
    sweep(pb, pa, src, 2, planes + 10, -1, 1.0)

    def restrict0(m, carry):
        both = leftover(pa, src, 2 * m + 6, -1, 1.0) + leftover(pa, src, 2 * m + 7, -1, 1.0)
        r1[m + PLANES_1, pl.ds(ROWS, rows1), :] = 0.125 * exact(
            down_y0[...], exact(both, down_z0[...])
        )
        return carry

    lax.fori_loop(0, planes1, restrict0, 0)
    copies = send_tiles(
        sizes,
        r1,
        r1,
        (planes1, rows1),
        PLANES_1,
        (send_sem.at[2], recv_sem.at[2]),
        origin=(PLANES_1, ROWS),
    )
    for copy in copies:
        copy.wait()

    def first1(i, carry):
        p1a[i] = (-4.0 * first_sweep) * r1[i]
        return carry

    lax.fori_loop(0, planes1 + 10, first1, 0)
    sweep(p1a, p1b, r1, 1, planes1 + 9, 0, 4.0)

    def restrict1(m, carry):
        both = leftover(p1b, r1, 2 * m + 3, 0, 4.0) + leftover(p1b, r1, 2 * m + 4, 0, 4.0)
        r2s[m] = 0.125 * exact(down_y1[...], exact(both, down_z1[...]))
        return carry

    lax.fori_loop(0, planes2 + 2, restrict1, 0)
    copies = []
    for way, (dx, dy) in enumerate(WAYS):
        from_x, count_x, to_x = {
            1: (0, PLANES_2, 0),
            -1: (1, PLANES_2, PLANES_2 + planes2),
            0: (1, planes2, PLANES_2),
        }[dx]
        from_y, count_y, to_y = part(dy, rows2, ROWS)
        copies.append(
            pltpu.make_async_remote_copy(
                src_ref=r2s.at[pl.ds(from_x, count_x), pl.ds(from_y, count_y)],
                dst_ref=r2.at[pl.ds(to_x, count_x), pl.ds(to_y, count_y)],
                send_sem=send_sem.at[3, way],
                recv_sem=recv_sem.at[3, way],
                device_id=neighbour(sizes, dx, dy),
                device_id_type=MESH,
            )
        )
    for copy in copies:
        copy.start()
    for k in range(planes2):
        r2[PLANES_2 + k, pl.ds(ROWS, rows2), :] = r2s[k + 1]
    for copy in copies:
        copy.wait()

    def first2(i, carry):
        c2a[i] = (-16.0 * first_sweep) * r2[i]
        return carry

    lax.fori_loop(0, planes2 + 10, first2, 0)
    sweep(c2a, c2b, r2, 1, planes2 + 9, 0, 16.0)
    sweep(c2b, c2a, r2, 2, planes2 + 8, 0, 16.0)
    sweep(c2a, c2b, r2, 3, planes2 + 7, 0, 16.0)

    def prolong1(m, carry):
        value = exact(up_y1[...], exact(c2b[m + 3], up_z1[...]))
        p1b[2 * m + 1] = p1b[2 * m + 1] + value
        p1b[2 * m + 2] = p1b[2 * m + 2] + value
        return carry

    lax.fori_loop(0, planes2 + 4, prolong1, 0)
    sweep(p1b, p1a, r1, 2, planes1 + 8, 0, 4.0)
    sweep(p1a, p1b, r1, 3, planes1 + 7, 0, 4.0)

    def prolong0(m, carry):
        value = exact(up_y0[...], exact(p1b[m + 3], up_z0[...]))
        pa[2 * m + 2] = pa[2 * m + 2] + value
        pa[2 * m + 3] = pa[2 * m + 3] + value
        return carry

    lax.fori_loop(0, planes1 + 4, prolong0, 0)
    sweep(pa, pb, src, 3, planes + 9, -1, 1.0)
    sweep(pb, pa, src, 4, planes + 8, -1, 1.0)

    def finish(k, carry):
        out[0, k] = pa[k + 6, pl.ds(ROWS, rows), :]
        ahead = pa[k + 7, pl.ds(ROWS, rows), :] - pa[k + 5, pl.ds(ROWS, rows), :]
        further = pa[k + 8, pl.ds(ROWS, rows), :] - pa[k + 4, pl.ds(ROWS, rows), :]
        out[1, k] = (8.0 * ahead - further) * (1.0 / 12.0)
        return carry

    lax.fori_loop(0, planes, finish, 0)


def pairing(fine, coarse, fine_halo, coarse_halo, wrap=0):
    fine_at = np.arange(fine) - fine_halo
    coarse_at = np.arange(coarse) - coarse_halo
    if wrap:
        coarse_at = coarse_at % wrap
    return (fine_at[None, :] // 2 == coarse_at[:, None]).astype(np.float32)


def v_cycle(fields, pressure, sizes):
    _, planes, rows, depth = fields.shape
    planes1, rows1, depth1 = planes // 2, rows // 2, depth // 2
    planes2, rows2, depth2 = planes // 4, rows // 4, depth // 4
    down_y0 = pairing(rows + 16, rows1, 8, 0)
    down_z0 = pairing(depth, depth1, 0, 0).T
    down_y1 = pairing(rows1 + 16, rows2, 8, 0)
    down_z1 = pairing(depth1, depth1, 0, 0, depth2).T
    up_y1 = pairing(rows1 + 16, rows2 + 16, 8, 8).T
    up_z1 = pairing(depth1, depth1, 0, 0)
    up_y0 = pairing(rows + 16, rows1 + 16, 8, 8).T
    up_z0 = pairing(depth, depth1, 0, 0)
    tables = [down_y0, down_z0, down_y1, down_z1, up_y1, up_z1, up_y0, up_z0]

    def vmem(count, height, width):
        return pltpu.VMEM((count, height, width), jnp.float32)

    return pl.pallas_call(
        functools.partial(cycle_kernel, sizes),
        out_shape=jax.ShapeDtypeStruct((2, planes, rows, depth), jnp.float32),
        in_specs=[pl.BlockSpec(memory_space=pl.ANY)] * 2
        + [pl.BlockSpec(memory_space=pltpu.VMEM)] * len(tables),
        out_specs=pl.BlockSpec(memory_space=pltpu.VMEM),
        scratch_shapes=[
            vmem(planes + 12, rows + 16, depth),
            vmem(planes + 12, rows + 16, depth),
            vmem(planes + 10, rows + 16, depth),
            vmem(planes + 14, rows + 16, depth),
            vmem(planes1 + 10, rows1 + 16, depth1),
            vmem(planes1 + 10, rows1 + 16, depth1),
            vmem(planes1 + 10, rows1 + 16, depth1),
            vmem(planes2 + 2, rows2, depth1),
            vmem(planes2 + 10, rows2 + 16, depth1),
            vmem(planes2 + 10, rows2 + 16, depth1),
            vmem(planes2 + 10, rows2 + 16, depth1),
            pltpu.SemaphoreType.DMA((3,)),
            pltpu.SemaphoreType.DMA((4, 8)),
            pltpu.SemaphoreType.DMA((4, 8)),
        ],
        compiler_params=pltpu.CompilerParams(
            collective_id=2, has_side_effects=True, vmem_limit_bytes=40 * 2**20
        ),
        name="v_cycle",
    )(fields, pressure, *[jnp.asarray(table) for table in tables])


def local(sizes, velocity, obstacle, pressure):
    row_count = velocity.shape[2]
    depth_count = velocity.shape[3]
    rows_first, rows_second = compact_tables(row_count)
    depth_first, depth_second = compact_tables(depth_count)
    rows_both = np.concatenate([rows_first, rows_second], axis=0)
    depth_both = np.concatenate([depth_first, depth_second], axis=0)
    keep = 1.0 - obstacle.astype(jnp.float32)
    pressure_extended = pressure_halo(pressure, sizes)
    padded = halo_planes(velocity, 1)
    row_terms = along_rows(rows_both, velocity)
    depth_terms = along_depth(depth_both, velocity)
    transverse = (
        velocity[1] * row_terms[:, :, :row_count] + velocity[2] * depth_terms[..., :depth_count]
    )
    diffusion = row_terms[:, :, row_count:] + depth_terms[..., depth_count:]
    streamwise = -velocity[0] * stream_first(padded, 1) + viscosity * stream_second(padded, 1)
    tendency = streamwise - transverse + viscosity * diffusion
    star = (velocity + time_step * tendency) * keep
    transverse_source = along_rows(rows_first, star[1]) + along_depth(depth_first, star[2])
    fields = lax.all_to_all(
        jnp.stack([star[0], transverse_source]), "group", split_axis=2, concat_axis=1, tiled=True
    )
    result = v_cycle(fields, pressure_extended, sizes)
    returned = lax.all_to_all(result, "group", split_axis=1, concat_axis=2, tiled=True)
    gradient = jnp.stack(
        [returned[1], along_rows(rows_first, returned[0]), along_depth(depth_first, returned[0])]
    )
    corrected = (star - gradient) * keep
    return (corrected, result[0])


def solution(mesh):
    in_specs = (
        P(None, ("tunnel", "group"), None, None),
        P(("tunnel", "group"), None, None),
        P("tunnel", "group", None),
    )
    out_specs = (P(None, ("tunnel", "group"), None, None), P("tunnel", "group", None))
    sizes = (mesh.shape["tunnel"], mesh.shape["group"])
    return jax.shard_map(
        functools.partial(local, sizes),
        mesh=mesh,
        in_specs=in_specs,
        out_specs=out_specs,
        check_vma=False,
    )
```

```python
import functools
import math

import jax
import jax.numpy as jnp
import numpy as np
from jax import lax
from jax.experimental import pallas as pl
from jax.experimental.pallas import tpu as pltpu
from jax.sharding import PartitionSpec as P

time_step = 0.1
viscosity = 0.05
relax_weight = 0.8
high = lax.Precision.HIGH
highest = lax.Precision.HIGHEST
MESH = pl.DeviceIdType.MESH

ROWS = 8
PLANES_P = 6
PLANES_U = 7
PLANES_S = 5
PLANES_1 = 5
PLANES_2 = 5
WAYS = [(dx, dy) for dx in (-1, 0, 1) for dy in (-1, 0, 1) if (dx, dy) != (0, 0)]


def compact_tables(count):
    indices = np.arange(count)
    angles = (indices[:, None] * indices[None, :] % count) * (2.0 * math.pi / count)
    cosines = np.cos(angles)
    sines = np.sin(angles)
    theta = indices * (2.0 * math.pi / count)
    first_wave = (14.0 / 9.0 * np.sin(theta) + np.sin(2.0 * theta) / 18.0) / (
        1.0 + 2.0 / 3.0 * np.cos(theta)
    )
    second_wave = (
        24.0 / 11.0 * (1.0 - np.cos(theta)) + 3.0 / 22.0 * (1.0 - np.cos(2.0 * theta))
    ) / (1.0 + 4.0 / 11.0 * np.cos(theta))
    first = ((cosines * first_wave) @ sines.T - (sines * first_wave) @ cosines.T) / count
    second = -((cosines * second_wave) @ cosines.T + (sines * second_wave) @ sines.T) / count
    return first.astype(np.float32), second.astype(np.float32)


def along_rows(matrix, field):
    return jnp.einsum("ij,...jz->...iz", matrix, field, precision=high)


def along_depth(matrix, field):
    return jnp.einsum("...j,ij->...i", field, matrix, precision=high)


def shifted(padded, offset, axis):
    count = padded.shape[axis] - 4
    return lax.slice_in_dim(padded, 2 + offset, 2 + offset + count, axis=axis)


def stream_first(padded, axis):
    ahead = shifted(padded, 1, axis) - shifted(padded, -1, axis)
    further = shifted(padded, 2, axis) - shifted(padded, -2, axis)
    return (8.0 * ahead - further) / 12.0


def stream_second(padded, axis):
    ahead = shifted(padded, 1, axis) + shifted(padded, -1, axis)
    further = shifted(padded, 2, axis) + shifted(padded, -2, axis)
    return (16.0 * ahead - further - 30.0 * shifted(padded, 0, axis)) / 12.0


def halo_planes(value, axis):
    size = lax.axis_size(("tunnel", "group"))
    up = [(i, (i + 1) % size) for i in range(size)]
    down = [(j, i) for i, j in up]
    before = lax.ppermute(value, ("tunnel", "group"), up)
    after = lax.ppermute(value, ("tunnel", "group"), down)
    return jnp.concatenate([before, value, after], axis=axis)


def part(step, length, halo):
    if step > 0:
        return length - halo, halo, 0
    if step < 0:
        return 0, halo, halo + length
    return 0, length, halo


def neighbour(sizes, dx, dy):
    me_x = lax.axis_index("tunnel")
    me_y = lax.axis_index("group")
    return (
        lax.rem(me_x + (dx + sizes[0]), sizes[0]),
        lax.rem(me_y + (dy + sizes[1]), sizes[1]),
    )


def enter(sizes):
    barrier = pltpu.get_barrier_semaphore()
    for dx, dy in WAYS:
        pl.semaphore_signal(
            barrier, inc=1, device_id=neighbour(sizes, dx, dy), device_id_type=MESH
        )
    pl.semaphore_wait(barrier, len(WAYS))


def send_tiles(sizes, source, target, shape, planes, sems, origin=(0, 0), lend=0):
    copies = []
    for way, (dx, dy) in enumerate(WAYS):
        from_x, count_x, to_x = part(dx, shape[0], planes)
        from_y, count_y, to_y = part(dy, shape[1], ROWS)
        if dx > 0:
            from_x = shape[0] + lend - planes if lend else from_x
        copies.append(
            pltpu.make_async_remote_copy(
                src_ref=source.at[
                    pl.ds(origin[0] + from_x, count_x), pl.ds(origin[1] + from_y, count_y)
                ],
                dst_ref=target.at[pl.ds(to_x, count_x), pl.ds(to_y, count_y)],
                send_sem=sems[0].at[way],
                recv_sem=sems[1].at[way],
                device_id=neighbour(sizes, dx, dy),
                device_id_type=MESH,
            )
        )
    for copy in copies:
        copy.start()
    return copies


def pressure_kernel(sizes, tile, extended, local_sem, send_sem, recv_sem):
    planes, rows, _ = tile.shape
    own = pltpu.make_async_copy(
        tile, extended.at[pl.ds(PLANES_P, planes), pl.ds(ROWS, rows)], local_sem
    )
    own.start()
    enter(sizes)
    copies = send_tiles(
        sizes, tile, extended, (planes, rows), PLANES_P, (send_sem, recv_sem)
    )
    own.wait()
    for copy in copies:
        copy.wait()


def pressure_halo(pressure, sizes):
    planes, rows, depth = pressure.shape
    return pl.pallas_call(
        functools.partial(pressure_kernel, sizes),
        out_shape=jax.ShapeDtypeStruct(
            (planes + 2 * PLANES_P, rows + 2 * ROWS, depth), jnp.float32
        ),
        in_specs=[pl.BlockSpec(memory_space=pl.ANY)],
        out_specs=pl.BlockSpec(memory_space=pl.ANY),
        scratch_shapes=[
            pltpu.SemaphoreType.DMA,
            pltpu.SemaphoreType.DMA((8,)),
            pltpu.SemaphoreType.DMA((8,)),
        ],
        compiler_params=pltpu.CompilerParams(collective_id=1, has_side_effects=True),
        name="pressure_halo",
    )(pressure)


def loop(start, stop, body, unroll=4):
    whole = (stop - start) // unroll

    def several(step, carry):
        for lane in range(unroll):
            body(start + step * unroll + lane)
        return carry

    if whole:
        lax.fori_loop(0, whole, several, 0)
    for index in range(start + whole * unroll, stop):
        body(index)


def around(value):
    rows, depth = value.shape
    total = pltpu.roll(value, 1, 0) + pltpu.roll(value, rows - 1, 0)
    return total + pltpu.roll(value, 1, 1) + pltpu.roll(value, depth - 1, 1)


def sweep(source, target, right, start, stop, offset, scale):
    weight = relax_weight / 6.0

    def body(i):
        mid = source[i]
        total = source[i + 1] + source[i - 1] + around(mid)
        if scale == 1.0:
            total = total - right[i + offset]
        else:
            total = total - scale * right[i + offset]
        target[i] = (1.0 - relax_weight) * mid + weight * total

    loop(start, stop, body)


def own_rows(source, i, rows):
    span = source[i]
    rolled = pltpu.roll(span, 1, 0) + pltpu.roll(span, rows + 2 * ROWS - 1, 0)
    inside = pl.ds(ROWS, rows)
    mid = source[i, inside, :]
    total = source[i + 1, inside, :] + source[i - 1, inside, :] + rolled[ROWS : ROWS + rows]
    depth = mid.shape[1]
    return total + pltpu.roll(mid, 1, 1) + pltpu.roll(mid, depth - 1, 1), mid


def leftover(source, right, i, offset, scale, rows):
    total, mid = own_rows(source, i, rows)
    return right[i + offset, pl.ds(ROWS, rows), :] - (total - 6.0 * mid) * (1.0 / scale)


def spread(value, table):
    upper = value.astype(jnp.bfloat16)
    lower = (value - upper.astype(jnp.float32)).astype(jnp.bfloat16)
    return jnp.dot(upper, table, preferred_element_type=jnp.float32) + jnp.dot(
        lower, table, preferred_element_type=jnp.float32
    )


def cycle_kernel(
    sizes,
    fields,
    pressure,
    down_z0,
    down_z1,
    up_z1,
    up_z0,
    out,
    pa,
    pb,
    src,
    star,
    fine0,
    half0,
    r1,
    p1a,
    p1b,
    fine1,
    half1,
    r2s,
    r2,
    c2a,
    c2b,
    tall1,
    rise1,
    tall0,
    rise0,
    local_sem,
    send_sem,
    recv_sem,
):
    _, planes, rows, depth = fields.shape
    planes1, rows1, depth1 = planes // 2, rows // 2, depth // 2
    planes2, rows2 = planes // 4, rows // 4
    weight = relax_weight / 6.0
    near, far = 2, PLANES_S - 2

    def copies_of(group, pieces):
        made = []
        for way, (source, target, dx, dy) in enumerate(pieces):
            made.append(
                pltpu.make_async_remote_copy(
                    src_ref=source,
                    dst_ref=target,
                    send_sem=send_sem.at[group, way],
                    recv_sem=recv_sem.at[group, way],
                    device_id=neighbour(sizes, dx, dy),
                    device_id_type=MESH,
                )
            )
        for copy in made:
            copy.start()
        return made

    def finished(copies):
        for copy in copies:
            copy.wait()

    own_star = pltpu.make_async_copy(fields.at[0], star.at[pl.ds(2, planes)], local_sem.at[0])
    own_src = pltpu.make_async_copy(
        fields.at[1], src.at[pl.ds(PLANES_S, planes), pl.ds(ROWS, rows)], local_sem.at[1]
    )
    own_pressure = pltpu.make_async_copy(pressure, pa, local_sem.at[2])
    own_star.start()
    own_src.start()
    own_pressure.start()
    enter(sizes)
    star_copies = copies_of(
        0,
        [
            (fields.at[0, pl.ds(planes - 2, 2)], star.at[pl.ds(0, 2)], 1, 0),
            (fields.at[0, pl.ds(0, 2)], star.at[pl.ds(planes + 2, 2)], -1, 0),
        ],
    )
    own_star.wait()
    own_src.wait()
    finished(star_copies)

    def divergence(k):
        inside = pl.ds(ROWS, rows)
        ahead = star[k + 3] - star[k + 1]
        further = star[k + 4] - star[k]
        src[k + PLANES_S, inside, :] = src[k + PLANES_S, inside, :] + (
            8.0 * ahead - further
        ) * (1.0 / 12.0)

    loop(0, planes, divergence)

    def source_piece(dx, dy, shift, count):
        if dx > 0:
            from_x, to_x = PLANES_S + planes - shift - count, PLANES_S - shift - count
        elif dx < 0:
            from_x, to_x = PLANES_S + shift, PLANES_S + planes + shift
        else:
            from_x, to_x, count = PLANES_S, PLANES_S, planes
        from_y, count_y, to_y = part(dy, rows, ROWS)
        return (
            src.at[pl.ds(from_x, count), pl.ds(ROWS + from_y, count_y)],
            src.at[pl.ds(to_x, count), pl.ds(to_y, count_y)],
            dx,
            dy,
        )

    near_copies = copies_of(1, [source_piece(dx, dy, 0, near) for dx, dy in WAYS])
    far_copies = copies_of(2, [source_piece(dx, dy, near, far) for dx, dy in WAYS if dx])
    own_pressure.wait()
    finished(near_copies)

    sweep(pa, pb, src, 4, planes + 8, -1, 1.0)
    sweep(pb, pa, src, 5, planes + 7, -1, 1.0)

    def restrict0(m):
        fine0[m] = leftover(pa, src, 2 * m + 6, -1, 1.0, rows) + leftover(
            pa, src, 2 * m + 7, -1, 1.0, rows
        )

    loop(0, planes1, restrict0, 2)
    half0[...] = spread(
        fine0[...].reshape(planes1 * rows, depth), down_z0[...]
    ).reshape(planes1, rows, depth1)
    for m in range(planes1):
        r1[m + PLANES_1, pl.ds(ROWS, rows1), :] = 0.125 * (
            half0[m, pl.ds(0, rows1, stride=2), :] + half0[m, pl.ds(1, rows1, stride=2), :]
        )

    def residual_piece(dx, dy):
        from_x, count_x, to_x = part(dx, planes1, PLANES_1)
        from_y, count_y, to_y = part(dy, rows1, ROWS)
        return (
            r1.at[pl.ds(PLANES_1 + from_x, count_x), pl.ds(ROWS + from_y, count_y)],
            r1.at[pl.ds(to_x, count_x), pl.ds(to_y, count_y)],
            dx,
            dy,
        )

    coarse_copies = copies_of(3, [residual_piece(dx, dy) for dx, dy in WAYS])

    finished(far_copies)
    sweep(pa, pb, src, 1, 4, -1, 1.0)
    sweep(pa, pb, src, planes + 8, planes + 11, -1, 1.0)
    sweep(pb, pa, src, 2, 5, -1, 1.0)
    sweep(pb, pa, src, planes + 7, planes + 10, -1, 1.0)
    finished(coarse_copies)

    p1a[...] = (-4.0 * weight) * r1[...]
    sweep(p1a, p1b, r1, 1, planes1 + 9, 0, 4.0)

    def restrict1(m):
        fine1[m] = leftover(p1b, r1, 2 * m + 3, 0, 4.0, rows1) + leftover(
            p1b, r1, 2 * m + 4, 0, 4.0, rows1
        )

    loop(0, planes2 + 2, restrict1, 2)
    half1[...] = spread(
        fine1[...].reshape((planes2 + 2) * rows1, depth1), down_z1[...]
    ).reshape(planes2 + 2, rows1, depth1)
    for m in range(planes2 + 2):
        value = 0.125 * (
            half1[m, pl.ds(0, rows2, stride=2), :] + half1[m, pl.ds(1, rows2, stride=2), :]
        )
        r2s[m] = value
        if 0 < m <= planes2:
            r2[m + PLANES_2 - 1, pl.ds(ROWS, rows2), :] = value

    def coarsest_piece(dx, dy):
        from_x, count_x, to_x = {
            1: (0, PLANES_2, 0),
            -1: (1, PLANES_2, PLANES_2 + planes2),
            0: (1, planes2, PLANES_2),
        }[dx]
        from_y, count_y, to_y = part(dy, rows2, ROWS)
        return (
            r2s.at[pl.ds(from_x, count_x), pl.ds(from_y, count_y)],
            r2.at[pl.ds(to_x, count_x), pl.ds(to_y, count_y)],
            dx,
            dy,
        )

    finished(copies_of(4, [coarsest_piece(dx, dy) for dx, dy in WAYS]))

    c2a[...] = (-16.0 * weight) * r2[...]
    sweep(c2a, c2b, r2, 1, planes2 + 9, 0, 16.0)
    sweep(c2b, c2a, r2, 2, planes2 + 8, 0, 16.0)
    sweep(c2a, c2b, r2, 3, planes2 + 7, 0, 16.0)

    def prolong(coarse, count, tall, wide, table):
        half = tall.shape[1] // 2
        for m in range(count):
            value = coarse[m + 3, pl.ds(ROWS // 2, half), :]
            tall[m, pl.ds(0, half, stride=2), :] = value
            tall[m, pl.ds(1, half, stride=2), :] = value
        wide[...] = spread(
            tall[...].reshape(count * tall.shape[1], tall.shape[2]), table[...]
        ).reshape(wide.shape)

    def add_pair(fine, wide, m, first):
        value = wide[m]
        fine[first] = fine[first] + value
        fine[first + 1] = fine[first + 1] + value

    prolong(c2b, planes2 + 4, tall1, rise1, up_z1)
    loop(0, planes2 + 4, lambda m: add_pair(p1b, rise1, m, 2 * m + 1))
    sweep(p1b, p1a, r1, 2, planes1 + 8, 0, 4.0)
    sweep(p1a, p1b, r1, 3, planes1 + 7, 0, 4.0)

    prolong(p1b, planes1 + 4, tall0, rise0, up_z0)
    loop(0, planes1 + 4, lambda m: add_pair(pa, rise0, m, 2 * m + 2))
    sweep(pa, pb, src, 3, planes + 9, -1, 1.0)

    def last(i):
        total, mid = own_rows(pb, i, rows)
        total = total - src[i - 1, pl.ds(ROWS, rows), :]
        pa[i, pl.ds(ROWS, rows), :] = (1.0 - relax_weight) * mid + weight * total

    loop(4, planes + 8, last)

    def finish(k):
        inside = pl.ds(ROWS, rows)
        out[0, k] = pa[k + 6, inside, :]
        ahead = pa[k + 7, inside, :] - pa[k + 5, inside, :]
        further = pa[k + 8, inside, :] - pa[k + 4, inside, :]
        out[1, k] = (8.0 * ahead - further) * (1.0 / 12.0)

    loop(0, planes, finish)


def pairing(fine, coarse, wrap=0):
    coarse_at = np.arange(coarse)
    if wrap:
        coarse_at = coarse_at % wrap
    return (np.arange(fine)[:, None] // 2 == coarse_at[None, :]).astype(np.float32)


def v_cycle(fields, pressure, sizes):
    _, planes, rows, depth = fields.shape
    planes1, rows1, depth1 = planes // 2, rows // 2, depth // 2
    planes2, rows2, depth2 = planes // 4, rows // 4, depth // 4
    down_z0 = pairing(depth, depth1)
    down_z1 = pairing(depth1, depth1, depth2)
    up_z1 = pairing(depth1, depth1).T
    up_z0 = pairing(depth, depth1).T
    tables = [down_z0, down_z1, up_z1, up_z0]

    def vmem(count, height, width):
        return pltpu.VMEM((count, height, width), jnp.float32)

    return pl.pallas_call(
        functools.partial(cycle_kernel, sizes),
        out_shape=jax.ShapeDtypeStruct((2, planes, rows, depth), jnp.float32),
        in_specs=[pl.BlockSpec(memory_space=pl.ANY)] * 2
        + [pl.BlockSpec(memory_space=pltpu.VMEM)] * len(tables),
        out_specs=pl.BlockSpec(memory_space=pltpu.VMEM),
        scratch_shapes=[
            vmem(planes + 12, rows + 16, depth),
            vmem(planes + 12, rows + 16, depth),
            vmem(planes + 10, rows + 16, depth),
            vmem(planes + 4, rows, depth),
            vmem(planes1, rows, depth),
            vmem(planes1, rows, depth1),
            vmem(planes1 + 10, rows1 + 16, depth1),
            vmem(planes1 + 10, rows1 + 16, depth1),
            vmem(planes1 + 10, rows1 + 16, depth1),
            vmem(planes2 + 2, rows1, depth1),
            vmem(planes2 + 2, rows1, depth1),
            vmem(planes2 + 2, rows2, depth1),
            vmem(planes2 + 10, rows2 + 16, depth1),
            vmem(planes2 + 10, rows2 + 16, depth1),
            vmem(planes2 + 10, rows2 + 16, depth1),
            vmem(planes2 + 4, rows1 + 16, depth1),
            vmem(planes2 + 4, rows1 + 16, depth1),
            vmem(planes1 + 4, rows + 16, depth1),
            vmem(planes1 + 4, rows + 16, depth),
            pltpu.SemaphoreType.DMA((3,)),
            pltpu.SemaphoreType.DMA((5, 8)),
            pltpu.SemaphoreType.DMA((5, 8)),
        ],
        compiler_params=pltpu.CompilerParams(
            collective_id=2, has_side_effects=True, vmem_limit_bytes=48 * 2**20
        ),
        name="v_cycle",
    )(fields, pressure, *[jnp.asarray(table, jnp.bfloat16) for table in tables])


def local(sizes, velocity, obstacle, pressure):
    row_count = velocity.shape[2]
    depth_count = velocity.shape[3]
    rows_first, rows_second = compact_tables(row_count)
    depth_first, depth_second = compact_tables(depth_count)
    rows_both = np.concatenate([rows_first, rows_second], axis=0)
    depth_both = np.concatenate([depth_first, depth_second], axis=0)
    keep = 1.0 - obstacle.astype(jnp.float32)
    pressure_extended = pressure_halo(pressure, sizes)
    padded = halo_planes(velocity, 1)
    settled, pressure_extended = lax.optimization_barrier((velocity, pressure_extended))
    row_terms = along_rows(rows_both, settled)
    depth_terms = along_depth(depth_both, settled)
    transverse = (
        velocity[1] * row_terms[:, :, :row_count] + velocity[2] * depth_terms[..., :depth_count]
    )
    diffusion = row_terms[:, :, row_count:] + depth_terms[..., depth_count:]
    streamwise = -velocity[0] * stream_first(padded, 1) + viscosity * stream_second(padded, 1)
    tendency = streamwise - transverse + viscosity * diffusion
    star = (velocity + time_step * tendency) * keep
    transverse_source = along_rows(rows_first, star[1]) + along_depth(depth_first, star[2])
    fields = lax.all_to_all(
        jnp.stack([star[0], transverse_source]), "group", split_axis=2, concat_axis=1, tiled=True
    )
    result = v_cycle(fields, pressure_extended, sizes)
    returned = lax.all_to_all(result, "group", split_axis=1, concat_axis=2, tiled=True)
    gradient = jnp.stack(
        [returned[1], along_rows(rows_first, returned[0]), along_depth(depth_first, returned[0])]
    )
    corrected = (star - gradient) * keep
    return (corrected, result[0])


def solution(mesh):
    in_specs = (
        P(None, ("tunnel", "group"), None, None),
        P(("tunnel", "group"), None, None),
        P("tunnel", "group", None),
    )
    out_specs = (P(None, ("tunnel", "group"), None, None), P("tunnel", "group", None))
    sizes = (mesh.shape["tunnel"], mesh.shape["group"])
    return jax.shard_map(
        functools.partial(local, sizes),
        mesh=mesh,
        in_specs=in_specs,
        out_specs=out_specs,
        check_vma=False,
    )
```

```python
import functools
import math

import jax
import jax.numpy as jnp
import ml_dtypes
import numpy as np
from jax import lax
from jax.experimental import pallas as pl
from jax.experimental.pallas import tpu as pltpu
from jax.sharding import PartitionSpec as P

time_step = 0.1
viscosity = 0.05
relax_weight = 0.8
high = lax.Precision.HIGH
MESH = pl.DeviceIdType.MESH

ROWS = 8
PLANES_P = 6
PLANES_S = 5
PLANES_1 = 5
PLANES_2 = 5
WAYS = [(dx, dy) for dx in (-1, 0, 1) for dy in (-1, 0, 1) if (dx, dy) != (0, 0)]


def compact_tables(count):
    indices = np.arange(count)
    angles = (indices[:, None] * indices[None, :] % count) * (2.0 * math.pi / count)
    cosines = np.cos(angles)
    sines = np.sin(angles)
    theta = indices * (2.0 * math.pi / count)
    first_wave = (14.0 / 9.0 * np.sin(theta) + np.sin(2.0 * theta) / 18.0) / (
        1.0 + 2.0 / 3.0 * np.cos(theta)
    )
    second_wave = (
        24.0 / 11.0 * (1.0 - np.cos(theta)) + 3.0 / 22.0 * (1.0 - np.cos(2.0 * theta))
    ) / (1.0 + 4.0 / 11.0 * np.cos(theta))
    first = ((cosines * first_wave) @ sines.T - (sines * first_wave) @ cosines.T) / count
    second = -((cosines * second_wave) @ cosines.T + (sines * second_wave) @ sines.T) / count
    return first.astype(np.float32), second.astype(np.float32)


def along_rows(matrix, field):
    return jnp.einsum("ij,...jz->...iz", matrix, field, precision=high)


def along_depth(matrix, field):
    return jnp.einsum("...j,ij->...i", field, matrix, precision=high)


def part(step, length, halo):
    if step > 0:
        return length - halo, halo, 0
    if step < 0:
        return 0, halo, halo + length
    return 0, length, halo


def neighbour(sizes, dx, dy):
    me_x = lax.axis_index("tunnel")
    me_y = lax.axis_index("group")
    return (
        lax.rem(me_x + (dx + sizes[0]), sizes[0]),
        lax.rem(me_y + (dy + sizes[1]), sizes[1]),
    )


def along_stream(sizes, step):
    me_x = lax.axis_index("tunnel")
    me_y = lax.axis_index("group")
    if step > 0:
        carry = lax.div(me_y + 1, sizes[1])
        return lax.rem(me_x + carry, sizes[0]), lax.rem(me_y + 1, sizes[1])
    carry = lax.div(me_y + sizes[1] - 1, sizes[1])
    return (
        lax.rem(me_x + sizes[0] - 1 + carry, sizes[0]),
        lax.rem(me_y + sizes[1] - 1, sizes[1]),
    )


def member(sizes, ahead):
    return lax.axis_index("tunnel"), lax.rem(lax.axis_index("group") + ahead, sizes[1])


def enter(sizes):
    barrier = pltpu.get_barrier_semaphore()
    partners = [neighbour(sizes, dx, dy) for dx, dy in WAYS]
    partners += [along_stream(sizes, 1), along_stream(sizes, -1)]
    partners += [member(sizes, ahead) for ahead in range(1, sizes[1])]
    for partner in partners:
        pl.semaphore_signal(barrier, inc=1, device_id=partner, device_id_type=MESH)
    pl.semaphore_wait(barrier, len(partners))


def loop(start, stop, body, unroll=4):
    whole = (stop - start) // unroll

    def several(step, carry):
        for lane in range(unroll):
            body(start + step * unroll + lane)
        return carry

    if whole:
        lax.fori_loop(0, whole, several, 0)
    for index in range(start + whole * unroll, stop):
        body(index)


def around(value):
    rows, depth = value.shape
    total = pltpu.roll(value, 1, 0) + pltpu.roll(value, rows - 1, 0)
    return total + pltpu.roll(value, 1, 1) + pltpu.roll(value, depth - 1, 1)


def sweep(source, target, right, start, stop, offset, scale):
    weight = relax_weight / 6.0

    def body(i):
        mid = source[i]
        total = source[i + 1] + source[i - 1] + around(mid)
        if scale == 1.0:
            total = total - right[i + offset]
        else:
            total = total - scale * right[i + offset]
        target[i] = (1.0 - relax_weight) * mid + weight * total

    loop(start, stop, body)


def own_rows(source, i, rows):
    span = source[i]
    rolled = pltpu.roll(span, 1, 0) + pltpu.roll(span, rows + 2 * ROWS - 1, 0)
    inside = pl.ds(ROWS, rows)
    mid = source[i, inside, :]
    total = source[i + 1, inside, :] + source[i - 1, inside, :] + rolled[ROWS : ROWS + rows]
    depth = mid.shape[1]
    return total + pltpu.roll(mid, 1, 1) + pltpu.roll(mid, depth - 1, 1), mid


def leftover(source, right, i, offset, scale, rows):
    total, mid = own_rows(source, i, rows)
    return right[i + offset, pl.ds(ROWS, rows), :] - (total - 6.0 * mid) * (1.0 / scale)


def spread(value, table):
    upper = value.astype(jnp.bfloat16)
    lower = (value - upper.astype(jnp.float32)).astype(jnp.bfloat16)
    return jnp.dot(upper, table, preferred_element_type=jnp.float32) + jnp.dot(
        lower, table, preferred_element_type=jnp.float32
    )


def halves(value):
    upper = value.astype(jnp.bfloat16)
    return upper, (value - upper.astype(jnp.float32)).astype(jnp.bfloat16)


def product(a, b):
    return jnp.dot(a, b, preferred_element_type=jnp.float32)


def cycle_kernel(
    sizes,
    velocity,
    obstacle,
    pressure,
    rows_high,
    rows_low,
    depth_high,
    depth_low,
    down_z0,
    down_z1,
    up_z1,
    up_z0,
    star_out,
    out,
    vel,
    solid,
    left,
    right,
    base,
    stars,
    cross,
    high,
    low,
    pa,
    pb,
    src,
    star,
    fine0,
    half0,
    r1,
    p1a,
    p1b,
    fine1,
    half1,
    r2s,
    r2,
    c2a,
    c2b,
    tall1,
    rise1,
    tall0,
    rise0,
    local_sem,
    send_sem,
    recv_sem,
):
    _, planes, rows, depth = out.shape
    planes1, rows1, depth1 = planes // 2, rows // 2, depth // 2
    planes2, rows2 = planes // 4, rows // 4
    weight = relax_weight / 6.0
    near, far = 2, PLANES_S - 2
    thick, height = velocity.shape[1], velocity.shape[2]
    members = sizes[1]
    me_y = lax.axis_index("group")

    def copy_to(group, way, source, target, device):
        copy = pltpu.make_async_remote_copy(
            src_ref=source,
            dst_ref=target,
            send_sem=send_sem.at[group, way],
            recv_sem=recv_sem.at[group, way],
            device_id=device,
            device_id_type=MESH,
        )
        copy.start()
        return copy

    def copies_of(group, pieces):
        return [
            copy_to(group, way, source, target, neighbour(sizes, dx, dy))
            for way, (source, target, dx, dy) in enumerate(pieces)
        ]

    def finished(copies):
        for copy in copies:
            copy.wait()

    def here(source, target, index):
        copy = pltpu.make_async_copy(source, target, local_sem.at[index])
        copy.start()
        return copy

    own_vel = here(velocity, vel, 0)
    own_solid = here(obstacle, solid, 1)
    own_pressure = here(pressure, pa.at[pl.ds(PLANES_P, planes), pl.ds(ROWS, rows)], 2)
    enter(sizes)

    def pressure_piece(dx, dy):
        from_x, count_x, to_x = part(dx, planes, PLANES_P)
        from_y, count_y, to_y = part(dy, rows, ROWS)
        return (
            pressure.at[pl.ds(from_x, count_x), pl.ds(from_y, count_y)],
            pa.at[pl.ds(to_x, count_x), pl.ds(to_y, count_y)],
            dx,
            dy,
        )

    def send_planes(c):
        return [
            copy_to(6, 2 * c, velocity.at[c], left.at[c], along_stream(sizes, 1)),
            copy_to(6, 2 * c + 1, velocity.at[c], right.at[c], along_stream(sizes, -1)),
        ]

    pressure_copies = copies_of(5, [pressure_piece(dx, dy) for dx, dy in WAYS])
    u_copies = send_planes(0)
    own_vel.wait()

    def transverse(index, carry):
        c, p = lax.div(index, thick), lax.rem(index, thick)
        upper, lower = halves(vel[c, p])
        high[...] = upper
        low[...] = lower
        first, second = pl.ds(0, height), pl.ds(height, height)
        row_first = (
            product(rows_high[first, :], high[...])
            + product(rows_high[first, :], low[...])
            + product(rows_low[first, :], high[...])
        )
        row_second = (
            product(rows_high[second, :], high[...])
            + product(rows_high[second, :], low[...])
            + product(rows_low[second, :], high[...])
        )
        along = (
            product(high[...], depth_high[...])
            + product(low[...], depth_high[...])
            + product(high[...], depth_low[...])
        )
        advection = vel[1, p] * row_first + vel[2, p] * along[:, :depth]
        base[c, p] = vel[c, p] + time_step * (
            viscosity * (row_second + along[:, depth:]) - advection
        )
        return carry

    lax.fori_loop(0, 3 * thick, transverse, 0)
    own_solid.wait()

    def predict(c):
        near_planes = [left.at[c, 0], left.at[c, 1], vel.at[c, 0], vel.at[c, 1]]
        near_planes += [right.at[c, 0], right.at[c, 1]]

        def rows_of(k):
            at = pl.ds(pl.multiple_of(k * rows, rows), rows)
            f = [plane[at, :] for plane in near_planes]
            for p in range(thick):
                ahead, further = f[p + 3] - f[p + 1], f[p + 4] - f[p]
                slope = (8.0 * ahead - further) * (1.0 / 12.0)
                beside, beyond = f[p + 3] + f[p + 1], f[p + 4] + f[p]
                bend = (16.0 * beside - beyond - 30.0 * f[p + 2]) * (1.0 / 12.0)
                keep = 1.0 - solid[p, at, :].astype(jnp.float32)
                stars[c, p, at, :] = keep * (
                    base[c, p, at, :]
                    + time_step * (viscosity * bend - vel[0, p, at, :] * slope)
                )

        loop(0, height // rows, rows_of, 1)

    def slabs(group, source, target):
        copies = []
        for ahead in range(1, members):
            device = member(sizes, ahead)
            at = pl.ds(pl.multiple_of(device[1] * rows, rows), rows)
            copies.append(copy_to(group, ahead - 1, source(at), target, device))
        return copies

    mine = pl.ds(pl.multiple_of(me_y * rows, rows), rows)

    for copy in u_copies:
        copy.wait_send()
    v_copies = send_planes(1)
    for copy in u_copies:
        copy.wait_recv()
    predict(0)
    star_at = star.at[pl.ds(2 + me_y * thick, thick)]
    star_slabs = slabs(7, lambda at: stars.at[0, :, at, :], star_at)
    own_star = here(stars.at[0, :, mine, :], star_at, 3)

    for copy in v_copies:
        copy.wait_send()
    w_copies = send_planes(2)
    for copy in v_copies:
        copy.wait_recv()
    predict(1)
    for p in range(thick):
        upper, lower = halves(stars[1, p])
        high[...] = upper
        low[...] = lower
        first = pl.ds(0, height)
        cross[p] = (
            product(rows_high[first, :], high[...])
            + product(rows_high[first, :], low[...])
            + product(rows_low[first, :], high[...])
        )
    own_star.wait()
    finished(star_slabs)
    star_copies = copies_of(
        0,
        [
            (star.at[pl.ds(planes, 2)], star.at[pl.ds(0, 2)], 1, 0),
            (star.at[pl.ds(2, 2)], star.at[pl.ds(planes + 2, 2)], -1, 0),
        ],
    )

    finished(w_copies)
    predict(2)
    for p in range(thick):
        upper, lower = halves(stars[2, p])
        wave_high, wave_low = depth_high[:, pl.ds(0, depth)], depth_low[:, pl.ds(0, depth)]
        cross[p] = cross[p] + (
            product(upper, wave_high) + product(lower, wave_high) + product(upper, wave_low)
        )
    src_at = src.at[pl.ds(PLANES_S + me_y * thick, thick), pl.ds(ROWS, rows)]
    src_slabs = slabs(8, lambda at: cross.at[:, at, :], src_at)
    own_src = here(cross.at[:, mine, :], src_at, 4)
    star_copy = here(stars, star_out, 5)
    finished(star_copies)
    own_src.wait()
    finished(src_slabs)

    def divergence(k):
        inside = pl.ds(ROWS, rows)
        ahead = star[k + 3] - star[k + 1]
        further = star[k + 4] - star[k]
        src[k + PLANES_S, inside, :] = src[k + PLANES_S, inside, :] + (
            8.0 * ahead - further
        ) * (1.0 / 12.0)

    loop(0, planes, divergence)

    def source_piece(dx, dy, shift, count):
        if dx > 0:
            from_x, to_x = PLANES_S + planes - shift - count, PLANES_S - shift - count
        elif dx < 0:
            from_x, to_x = PLANES_S + shift, PLANES_S + planes + shift
        else:
            from_x, to_x, count = PLANES_S, PLANES_S, planes
        from_y, count_y, to_y = part(dy, rows, ROWS)
        return (
            src.at[pl.ds(from_x, count), pl.ds(ROWS + from_y, count_y)],
            src.at[pl.ds(to_x, count), pl.ds(to_y, count_y)],
            dx,
            dy,
        )

    near_copies = copies_of(1, [source_piece(dx, dy, 0, near) for dx, dy in WAYS])
    far_copies = copies_of(2, [source_piece(dx, dy, near, far) for dx, dy in WAYS if dx])
    own_pressure.wait()
    finished(pressure_copies)
    finished(near_copies)

    sweep(pa, pb, src, 4, planes + 8, -1, 1.0)
    sweep(pb, pa, src, 5, planes + 7, -1, 1.0)

    def restrict0(m):
        fine0[m] = leftover(pa, src, 2 * m + 6, -1, 1.0, rows) + leftover(
            pa, src, 2 * m + 7, -1, 1.0, rows
        )

    loop(0, planes1, restrict0, 2)
    half0[...] = spread(
        fine0[...].reshape(planes1 * rows, depth), down_z0[...]
    ).reshape(planes1, rows, depth1)
    for m in range(planes1):
        r1[m + PLANES_1, pl.ds(ROWS, rows1), :] = 0.125 * (
            half0[m, pl.ds(0, rows1, stride=2), :] + half0[m, pl.ds(1, rows1, stride=2), :]
        )

    def residual_piece(dx, dy):
        from_x, count_x, to_x = part(dx, planes1, PLANES_1)
        from_y, count_y, to_y = part(dy, rows1, ROWS)
        return (
            r1.at[pl.ds(PLANES_1 + from_x, count_x), pl.ds(ROWS + from_y, count_y)],
            r1.at[pl.ds(to_x, count_x), pl.ds(to_y, count_y)],
            dx,
            dy,
        )

    coarse_copies = copies_of(3, [residual_piece(dx, dy) for dx, dy in WAYS])

    finished(far_copies)
    sweep(pa, pb, src, 1, 4, -1, 1.0)
    sweep(pa, pb, src, planes + 8, planes + 11, -1, 1.0)
    sweep(pb, pa, src, 2, 5, -1, 1.0)
    sweep(pb, pa, src, planes + 7, planes + 10, -1, 1.0)
    finished(coarse_copies)

    p1a[...] = (-4.0 * weight) * r1[...]
    sweep(p1a, p1b, r1, 1, planes1 + 9, 0, 4.0)

    def restrict1(m):
        fine1[m] = leftover(p1b, r1, 2 * m + 3, 0, 4.0, rows1) + leftover(
            p1b, r1, 2 * m + 4, 0, 4.0, rows1
        )

    loop(0, planes2 + 2, restrict1, 2)
    half1[...] = spread(
        fine1[...].reshape((planes2 + 2) * rows1, depth1), down_z1[...]
    ).reshape(planes2 + 2, rows1, depth1)
    for m in range(planes2 + 2):
        value = 0.125 * (
            half1[m, pl.ds(0, rows2, stride=2), :] + half1[m, pl.ds(1, rows2, stride=2), :]
        )
        r2s[m] = value
        if 0 < m <= planes2:
            r2[m + PLANES_2 - 1, pl.ds(ROWS, rows2), :] = value

    def coarsest_piece(dx, dy):
        from_x, count_x, to_x = {
            1: (0, PLANES_2, 0),
            -1: (1, PLANES_2, PLANES_2 + planes2),
            0: (1, planes2, PLANES_2),
        }[dx]
        from_y, count_y, to_y = part(dy, rows2, ROWS)
        return (
            r2s.at[pl.ds(from_x, count_x), pl.ds(from_y, count_y)],
            r2.at[pl.ds(to_x, count_x), pl.ds(to_y, count_y)],
            dx,
            dy,
        )

    finished(copies_of(4, [coarsest_piece(dx, dy) for dx, dy in WAYS]))

    c2a[...] = (-16.0 * weight) * r2[...]
    sweep(c2a, c2b, r2, 1, planes2 + 9, 0, 16.0)
    sweep(c2b, c2a, r2, 2, planes2 + 8, 0, 16.0)
    sweep(c2a, c2b, r2, 3, planes2 + 7, 0, 16.0)

    def prolong(coarse, count, tall, wide, table):
        half = tall.shape[1] // 2
        for m in range(count):
            value = coarse[m + 3, pl.ds(ROWS // 2, half), :]
            tall[m, pl.ds(0, half, stride=2), :] = value
            tall[m, pl.ds(1, half, stride=2), :] = value
        wide[...] = spread(
            tall[...].reshape(count * tall.shape[1], tall.shape[2]), table[...]
        ).reshape(wide.shape)

    def add_pair(fine, wide, m, first):
        value = wide[m]
        fine[first] = fine[first] + value
        fine[first + 1] = fine[first + 1] + value

    prolong(c2b, planes2 + 4, tall1, rise1, up_z1)
    loop(0, planes2 + 4, lambda m: add_pair(p1b, rise1, m, 2 * m + 1))
    sweep(p1b, p1a, r1, 2, planes1 + 8, 0, 4.0)
    sweep(p1a, p1b, r1, 3, planes1 + 7, 0, 4.0)

    prolong(p1b, planes1 + 4, tall0, rise0, up_z0)
    loop(0, planes1 + 4, lambda m: add_pair(pa, rise0, m, 2 * m + 2))
    sweep(pa, pb, src, 3, planes + 9, -1, 1.0)

    def last(i):
        total, mid = own_rows(pb, i, rows)
        total = total - src[i - 1, pl.ds(ROWS, rows), :]
        pa[i, pl.ds(ROWS, rows), :] = (1.0 - relax_weight) * mid + weight * total

    loop(4, planes + 8, last)

    def finish(k):
        inside = pl.ds(ROWS, rows)
        out[0, k] = pa[k + 6, inside, :]
        ahead = pa[k + 7, inside, :] - pa[k + 5, inside, :]
        further = pa[k + 8, inside, :] - pa[k + 4, inside, :]
        out[1, k] = (8.0 * ahead - further) * (1.0 / 12.0)

    loop(0, planes, finish)
    star_copy.wait()


def pairing(fine, coarse, wrap=0):
    coarse_at = np.arange(coarse)
    if wrap:
        coarse_at = coarse_at % wrap
    return (np.arange(fine)[:, None] // 2 == coarse_at[None, :]).astype(np.float32)


def two_parts(table):
    upper = table.astype(ml_dtypes.bfloat16)
    lower = (table - upper.astype(np.float32)).astype(ml_dtypes.bfloat16)
    return [jnp.asarray(upper), jnp.asarray(lower)]


def predict_and_cycle(velocity, obstacle, pressure, row_tables, depth_tables, sizes):
    planes, rows, depth = pressure.shape
    _, thick, height, _ = velocity.shape
    planes1, rows1, depth1 = planes // 2, rows // 2, depth // 2
    planes2, rows2, depth2 = planes // 4, rows // 4, depth // 4
    down_z0 = pairing(depth, depth1)
    down_z1 = pairing(depth1, depth1, depth2)
    up_z1 = pairing(depth1, depth1).T
    up_z0 = pairing(depth, depth1).T
    tables = two_parts(np.concatenate(row_tables, axis=0))
    tables += two_parts(np.concatenate([table.T for table in depth_tables], axis=1))
    tables += [
        jnp.asarray(table, jnp.bfloat16) for table in (down_z0, down_z1, up_z1, up_z0)
    ]

    def vmem(*shape):
        return pltpu.VMEM(shape, jnp.float32)

    return pl.pallas_call(
        functools.partial(cycle_kernel, sizes),
        out_shape=(
            jax.ShapeDtypeStruct(velocity.shape, jnp.float32),
            jax.ShapeDtypeStruct((2, planes, rows, depth), jnp.float32),
        ),
        in_specs=[pl.BlockSpec(memory_space=pl.ANY)] * 3
        + [pl.BlockSpec(memory_space=pltpu.VMEM)] * len(tables),
        out_specs=(
            pl.BlockSpec(memory_space=pl.ANY),
            pl.BlockSpec(memory_space=pltpu.VMEM),
        ),
        scratch_shapes=[
            vmem(3, thick, height, depth),
            pltpu.VMEM((thick, height, depth), jnp.int32),
            vmem(3, thick, height, depth),
            vmem(3, thick, height, depth),
            vmem(3, thick, height, depth),
            vmem(3, thick, height, depth),
            vmem(thick, height, depth),
            pltpu.VMEM((height, depth), jnp.bfloat16),
            pltpu.VMEM((height, depth), jnp.bfloat16),
            vmem(planes + 12, rows + 16, depth),
            vmem(planes + 12, rows + 16, depth),
            vmem(planes + 10, rows + 16, depth),
            vmem(planes + 4, rows, depth),
            vmem(planes1, rows, depth),
            vmem(planes1, rows, depth1),
            vmem(planes1 + 10, rows1 + 16, depth1),
            vmem(planes1 + 10, rows1 + 16, depth1),
            vmem(planes1 + 10, rows1 + 16, depth1),
            vmem(planes2 + 2, rows1, depth1),
            vmem(planes2 + 2, rows1, depth1),
            vmem(planes2 + 2, rows2, depth1),
            vmem(planes2 + 10, rows2 + 16, depth1),
            vmem(planes2 + 10, rows2 + 16, depth1),
            vmem(planes2 + 10, rows2 + 16, depth1),
            vmem(planes2 + 4, rows1 + 16, depth1),
            vmem(planes2 + 4, rows1 + 16, depth1),
            vmem(planes1 + 4, rows + 16, depth1),
            vmem(planes1 + 4, rows + 16, depth),
            pltpu.SemaphoreType.DMA((6,)),
            pltpu.SemaphoreType.DMA((9, 8)),
            pltpu.SemaphoreType.DMA((9, 8)),
        ],
        compiler_params=pltpu.CompilerParams(
            collective_id=1, has_side_effects=True, vmem_limit_bytes=56 * 2**20
        ),
        name="predict_and_cycle",
    )(velocity, obstacle, pressure, *tables)


def local(sizes, velocity, obstacle, pressure):
    row_tables = compact_tables(velocity.shape[2])
    depth_tables = compact_tables(velocity.shape[3])
    keep = 1.0 - obstacle.astype(jnp.float32)
    star, result = predict_and_cycle(
        velocity, obstacle, pressure, row_tables, depth_tables, sizes
    )
    returned = lax.all_to_all(result, "group", split_axis=1, concat_axis=2, tiled=True)
    gradient = jnp.stack(
        [
            returned[1],
            along_rows(row_tables[0], returned[0]),
            along_depth(depth_tables[0], returned[0]),
        ]
    )
    corrected = (star - gradient) * keep
    return (corrected, result[0])


def solution(mesh):
    in_specs = (
        P(None, ("tunnel", "group"), None, None),
        P(("tunnel", "group"), None, None),
        P("tunnel", "group", None),
    )
    out_specs = (P(None, ("tunnel", "group"), None, None), P("tunnel", "group", None))
    sizes = (mesh.shape["tunnel"], mesh.shape["group"])
    return jax.shard_map(
        functools.partial(local, sizes),
        mesh=mesh,
        in_specs=in_specs,
        out_specs=out_specs,
        check_vma=False,
    )
```

```python
import functools
import math

import jax
import jax.numpy as jnp
import ml_dtypes
import numpy as np
from jax import lax
from jax.experimental import pallas as pl
from jax.experimental.pallas import tpu as pltpu
from jax.sharding import PartitionSpec as P

time_step = 0.1
viscosity = 0.05
relax_weight = 0.8
high = lax.Precision.HIGH
MESH = pl.DeviceIdType.MESH

ROWS = 8
PLANES_P = 6
PLANES_S = 5
PLANES_1 = 5
PLANES_2 = 5
WAYS = [(dx, dy) for dx in (-1, 0, 1) for dy in (-1, 0, 1) if (dx, dy) != (0, 0)]


def compact_tables(count):
    indices = np.arange(count)
    angles = (indices[:, None] * indices[None, :] % count) * (2.0 * math.pi / count)
    cosines = np.cos(angles)
    sines = np.sin(angles)
    theta = indices * (2.0 * math.pi / count)
    first_wave = (14.0 / 9.0 * np.sin(theta) + np.sin(2.0 * theta) / 18.0) / (
        1.0 + 2.0 / 3.0 * np.cos(theta)
    )
    second_wave = (
        24.0 / 11.0 * (1.0 - np.cos(theta)) + 3.0 / 22.0 * (1.0 - np.cos(2.0 * theta))
    ) / (1.0 + 4.0 / 11.0 * np.cos(theta))
    first = ((cosines * first_wave) @ sines.T - (sines * first_wave) @ cosines.T) / count
    second = -((cosines * second_wave) @ cosines.T + (sines * second_wave) @ sines.T) / count
    return first.astype(np.float32), second.astype(np.float32)


def along_rows(matrix, field):
    return jnp.einsum("ij,...jz->...iz", matrix, field, precision=high)


def along_depth(matrix, field):
    return jnp.einsum("...j,ij->...i", field, matrix, precision=high)


def part(step, length, halo):
    if step > 0:
        return length - halo, halo, 0
    if step < 0:
        return 0, halo, halo + length
    return 0, length, halo


def neighbour(sizes, dx, dy):
    me_x = lax.axis_index("tunnel")
    me_y = lax.axis_index("group")
    return (
        lax.rem(me_x + (dx + sizes[0]), sizes[0]),
        lax.rem(me_y + (dy + sizes[1]), sizes[1]),
    )


def stream_planes(value):
    size = lax.axis_size(("tunnel", "group"))
    up = [(i, (i + 1) % size) for i in range(size)]
    down = [(j, i) for i, j in up]
    before = lax.ppermute(value, ("tunnel", "group"), up)
    after = lax.ppermute(value, ("tunnel", "group"), down)
    return before, after


def member(sizes, ahead):
    return lax.axis_index("tunnel"), lax.rem(lax.axis_index("group") + ahead, sizes[1])


def enter(sizes):
    barrier = pltpu.get_barrier_semaphore()
    partners = [neighbour(sizes, dx, dy) for dx, dy in WAYS]
    partners += [member(sizes, ahead) for ahead in range(1, sizes[1])]
    for partner in partners:
        pl.semaphore_signal(barrier, inc=1, device_id=partner, device_id_type=MESH)
    pl.semaphore_wait(barrier, len(partners))


def loop(start, stop, body, unroll=4):
    whole = (stop - start) // unroll

    def several(step, carry):
        for lane in range(unroll):
            body(start + step * unroll + lane)
        return carry

    if whole:
        lax.fori_loop(0, whole, several, 0)
    for index in range(start + whole * unroll, stop):
        body(index)


def around(value):
    rows, depth = value.shape
    total = pltpu.roll(value, 1, 0) + pltpu.roll(value, rows - 1, 0)
    return total + pltpu.roll(value, 1, 1) + pltpu.roll(value, depth - 1, 1)


def sweep(source, target, right, start, stop, offset, scale):
    weight = relax_weight / 6.0

    def body(i):
        mid = source[i]
        total = source[i + 1] + source[i - 1] + around(mid)
        if scale == 1.0:
            total = total - right[i + offset]
        else:
            total = total - scale * right[i + offset]
        target[i] = (1.0 - relax_weight) * mid + weight * total

    loop(start, stop, body)


def own_rows(source, i, rows):
    span = source[i]
    rolled = pltpu.roll(span, 1, 0) + pltpu.roll(span, rows + 2 * ROWS - 1, 0)
    inside = pl.ds(ROWS, rows)
    mid = source[i, inside, :]
    total = source[i + 1, inside, :] + source[i - 1, inside, :] + rolled[ROWS : ROWS + rows]
    depth = mid.shape[1]
    return total + pltpu.roll(mid, 1, 1) + pltpu.roll(mid, depth - 1, 1), mid


def leftover(source, right, i, offset, scale, rows):
    total, mid = own_rows(source, i, rows)
    return right[i + offset, pl.ds(ROWS, rows), :] - (total - 6.0 * mid) * (1.0 / scale)


def spread(value, table):
    upper = value.astype(jnp.bfloat16)
    lower = (value - upper.astype(jnp.float32)).astype(jnp.bfloat16)
    return jnp.dot(upper, table, preferred_element_type=jnp.float32) + jnp.dot(
        lower, table, preferred_element_type=jnp.float32
    )


def halves(value):
    upper = value.astype(jnp.bfloat16)
    return upper, (value - upper.astype(jnp.float32)).astype(jnp.bfloat16)


def product(a, b):
    return jnp.dot(a, b, preferred_element_type=jnp.float32)


def transverse_kernel(vel, rows_high, rows_low, depth_high, depth_low, base, high, low):
    height, depth = vel.shape[2], vel.shape[3]
    first, second = pl.ds(0, height), pl.ds(height, height)

    def component(c, carry):
        upper, lower = halves(vel[c, 0])
        high[...] = upper
        low[...] = lower
        row_first = (
            product(rows_high[first, :], high[...])
            + product(rows_high[first, :], low[...])
            + product(rows_low[first, :], high[...])
        )
        row_second = (
            product(rows_high[second, :], high[...])
            + product(rows_high[second, :], low[...])
            + product(rows_low[second, :], high[...])
        )
        along = (
            product(high[...], depth_high[...])
            + product(low[...], depth_high[...])
            + product(high[...], depth_low[...])
        )
        advection = vel[1, 0] * row_first + vel[2, 0] * along[:, :depth]
        base[c, 0] = vel[c, 0] + time_step * (
            viscosity * (row_second + along[:, depth:]) - advection
        )
        return carry

    lax.fori_loop(0, 3, component, 0)


def transverse(velocity, tables):
    _, thick, height, depth = velocity.shape
    plane = pl.BlockSpec((3, 1, height, depth), lambda p: (0, p, 0, 0))
    flops = 2 * 9 * thick * height * depth * 2 * (height + depth)
    return pl.pallas_call(
        transverse_kernel,
        grid=(thick,),
        out_shape=jax.ShapeDtypeStruct(velocity.shape, jnp.float32),
        in_specs=[plane] + [pl.BlockSpec(memory_space=pltpu.VMEM)] * 4,
        out_specs=plane,
        scratch_shapes=[pltpu.VMEM((height, depth), jnp.bfloat16)] * 2,
        compiler_params=pltpu.CompilerParams(vmem_limit_bytes=32 * 2**20),
        cost_estimate=pl.CostEstimate(
            flops=flops, bytes_accessed=8 * 3 * thick * height * depth, transcendentals=0
        ),
        name="transverse",
    )(velocity, *tables)


def cycle_kernel(
    sizes,
    velocity,
    before,
    after,
    across,
    obstacle,
    pressure,
    rows_high,
    rows_low,
    depth_high,
    depth_low,
    down_z0,
    down_z1,
    up_z1,
    up_z0,
    star_out,
    out,
    vel,
    solid,
    left,
    right,
    base,
    stars,
    cross,
    high,
    low,
    pa,
    pb,
    src,
    star,
    fine0,
    half0,
    r1,
    p1a,
    p1b,
    fine1,
    half1,
    r2s,
    r2,
    c2a,
    c2b,
    tall1,
    rise1,
    tall0,
    rise0,
    local_sem,
    send_sem,
    recv_sem,
):
    planes, _, rows, depth = out.shape
    planes1, rows1, depth1 = planes // 2, rows // 2, depth // 2
    planes2, rows2 = planes // 4, rows // 4
    weight = relax_weight / 6.0
    near, far = 2, PLANES_S - 2
    thick, height = velocity.shape[1], velocity.shape[2]
    members = sizes[1]
    me_y = lax.axis_index("group")

    def copy_to(group, way, source, target, device):
        copy = pltpu.make_async_remote_copy(
            src_ref=source,
            dst_ref=target,
            send_sem=send_sem.at[group, way],
            recv_sem=recv_sem.at[group, way],
            device_id=device,
            device_id_type=MESH,
        )
        copy.start()
        return copy

    def copies_of(group, pieces):
        return [
            copy_to(group, way, source, target, neighbour(sizes, dx, dy))
            for way, (source, target, dx, dy) in enumerate(pieces)
        ]

    def finished(copies):
        for copy in copies:
            copy.wait()

    def here(source, target, index):
        copy = pltpu.make_async_copy(source, target, local_sem.at[index])
        copy.start()
        return copy

    def load(c):
        pairs = [(velocity, vel), (before, left), (after, right), (across, base)]
        return [
            here(source.at[c], target.at[c], 6 + 4 * c + index)
            for index, (source, target) in enumerate(pairs)
        ]

    loads = [load(0)]
    own_solid = here(obstacle, solid, 1)
    loads += [load(1), load(2)]
    own_pressure = here(pressure, pa.at[pl.ds(PLANES_P, planes), pl.ds(ROWS, rows)], 2)
    enter(sizes)

    def pressure_piece(dx, dy):
        from_x, count_x, to_x = part(dx, planes, PLANES_P)
        from_y, count_y, to_y = part(dy, rows, ROWS)
        return (
            pressure.at[pl.ds(from_x, count_x), pl.ds(from_y, count_y)],
            pa.at[pl.ds(to_x, count_x), pl.ds(to_y, count_y)],
            dx,
            dy,
        )

    pressure_copies = copies_of(5, [pressure_piece(dx, dy) for dx, dy in WAYS])

    def predict(c):
        near_planes = [left.at[c, 0], left.at[c, 1], vel.at[c, 0], vel.at[c, 1]]
        near_planes += [right.at[c, 0], right.at[c, 1]]

        def rows_of(k):
            at = pl.ds(pl.multiple_of(k * rows, rows), rows)
            f = [plane[at, :] for plane in near_planes]
            for p in range(thick):
                ahead, further = f[p + 3] - f[p + 1], f[p + 4] - f[p]
                slope = (8.0 * ahead - further) * (1.0 / 12.0)
                beside, beyond = f[p + 3] + f[p + 1], f[p + 4] + f[p]
                bend = (16.0 * beside - beyond - 30.0 * f[p + 2]) * (1.0 / 12.0)
                keep = 1.0 - solid[p, at, :].astype(jnp.float32)
                stars[c, p, at, :] = keep * (
                    base[c, p, at, :]
                    + time_step * (viscosity * bend - vel[0, p, at, :] * slope)
                )

        loop(0, height // rows, rows_of, 1)

    def slabs(group, source, target):
        copies = []
        for ahead in range(1, members):
            device = member(sizes, ahead)
            at = pl.ds(pl.multiple_of(device[1] * rows, rows), rows)
            copies.append(copy_to(group, ahead - 1, source(at), target, device))
        return copies

    mine = pl.ds(pl.multiple_of(me_y * rows, rows), rows)

    finished(loads[0])
    own_solid.wait()
    predict(0)
    star_at = star.at[pl.ds(2 + me_y * thick, thick)]
    star_slabs = slabs(7, lambda at: stars.at[0, :, at, :], star_at)
    own_star = here(stars.at[0, :, mine, :], star_at, 3)

    finished(loads[1])
    predict(1)
    for p in range(thick):
        upper, lower = halves(stars[1, p])
        high[...] = upper
        low[...] = lower
        first = pl.ds(0, height)
        cross[p] = (
            product(rows_high[first, :], high[...])
            + product(rows_high[first, :], low[...])
            + product(rows_low[first, :], high[...])
        )
    finished(loads[2])
    predict(2)
    for p in range(thick):
        upper, lower = halves(stars[2, p])
        wave_high, wave_low = depth_high[:, pl.ds(0, depth)], depth_low[:, pl.ds(0, depth)]
        cross[p] = cross[p] + (
            product(upper, wave_high) + product(lower, wave_high) + product(upper, wave_low)
        )
    src_at = src.at[pl.ds(PLANES_S + me_y * thick, thick), pl.ds(ROWS, rows)]
    src_slabs = slabs(8, lambda at: cross.at[:, at, :], src_at)
    own_src = here(cross.at[:, mine, :], src_at, 4)
    star_copy = here(stars, star_out, 5)
    own_star.wait()
    finished(star_slabs)
    star_copies = copies_of(
        0,
        [
            (star.at[pl.ds(planes, 2)], star.at[pl.ds(0, 2)], 1, 0),
            (star.at[pl.ds(2, 2)], star.at[pl.ds(planes + 2, 2)], -1, 0),
        ],
    )

    finished(star_copies)
    own_src.wait()
    finished(src_slabs)

    def divergence(k):
        inside = pl.ds(ROWS, rows)
        ahead = star[k + 3] - star[k + 1]
        further = star[k + 4] - star[k]
        src[k + PLANES_S, inside, :] = src[k + PLANES_S, inside, :] + (
            8.0 * ahead - further
        ) * (1.0 / 12.0)

    loop(0, planes, divergence)

    def source_piece(dx, dy, shift, count):
        if dx > 0:
            from_x, to_x = PLANES_S + planes - shift - count, PLANES_S - shift - count
        elif dx < 0:
            from_x, to_x = PLANES_S + shift, PLANES_S + planes + shift
        else:
            from_x, to_x, count = PLANES_S, PLANES_S, planes
        from_y, count_y, to_y = part(dy, rows, ROWS)
        return (
            src.at[pl.ds(from_x, count), pl.ds(ROWS + from_y, count_y)],
            src.at[pl.ds(to_x, count), pl.ds(to_y, count_y)],
            dx,
            dy,
        )

    near_copies = copies_of(1, [source_piece(dx, dy, 0, near) for dx, dy in WAYS])
    far_copies = copies_of(2, [source_piece(dx, dy, near, far) for dx, dy in WAYS if dx])
    own_pressure.wait()
    finished(pressure_copies)
    finished(near_copies)

    sweep(pa, pb, src, 4, planes + 8, -1, 1.0)
    sweep(pb, pa, src, 5, planes + 7, -1, 1.0)

    def restrict0(m):
        fine0[m] = leftover(pa, src, 2 * m + 6, -1, 1.0, rows) + leftover(
            pa, src, 2 * m + 7, -1, 1.0, rows
        )

    loop(0, planes1, restrict0, 2)
    half0[...] = spread(
        fine0[...].reshape(planes1 * rows, depth), down_z0[...]
    ).reshape(planes1, rows, depth1)
    for m in range(planes1):
        r1[m + PLANES_1, pl.ds(ROWS, rows1), :] = 0.125 * (
            half0[m, pl.ds(0, rows1, stride=2), :] + half0[m, pl.ds(1, rows1, stride=2), :]
        )

    def residual_piece(dx, dy):
        from_x, count_x, to_x = part(dx, planes1, PLANES_1)
        from_y, count_y, to_y = part(dy, rows1, ROWS)
        return (
            r1.at[pl.ds(PLANES_1 + from_x, count_x), pl.ds(ROWS + from_y, count_y)],
            r1.at[pl.ds(to_x, count_x), pl.ds(to_y, count_y)],
            dx,
            dy,
        )

    coarse_copies = copies_of(3, [residual_piece(dx, dy) for dx, dy in WAYS])

    finished(far_copies)
    sweep(pa, pb, src, 1, 4, -1, 1.0)
    sweep(pa, pb, src, planes + 8, planes + 11, -1, 1.0)
    sweep(pb, pa, src, 2, 5, -1, 1.0)
    sweep(pb, pa, src, planes + 7, planes + 10, -1, 1.0)
    finished(coarse_copies)

    p1a[...] = (-4.0 * weight) * r1[...]
    sweep(p1a, p1b, r1, 1, planes1 + 9, 0, 4.0)

    def restrict1(m):
        fine1[m] = leftover(p1b, r1, 2 * m + 3, 0, 4.0, rows1) + leftover(
            p1b, r1, 2 * m + 4, 0, 4.0, rows1
        )

    loop(0, planes2 + 2, restrict1, 2)
    half1[...] = spread(
        fine1[...].reshape((planes2 + 2) * rows1, depth1), down_z1[...]
    ).reshape(planes2 + 2, rows1, depth1)
    for m in range(planes2 + 2):
        value = 0.125 * (
            half1[m, pl.ds(0, rows2, stride=2), :] + half1[m, pl.ds(1, rows2, stride=2), :]
        )
        r2s[m] = value
        if 0 < m <= planes2:
            r2[m + PLANES_2 - 1, pl.ds(ROWS, rows2), :] = value

    def coarsest_piece(dx, dy):
        from_x, count_x, to_x = {
            1: (0, PLANES_2, 0),
            -1: (1, PLANES_2, PLANES_2 + planes2),
            0: (1, planes2, PLANES_2),
        }[dx]
        from_y, count_y, to_y = part(dy, rows2, ROWS)
        return (
            r2s.at[pl.ds(from_x, count_x), pl.ds(from_y, count_y)],
            r2.at[pl.ds(to_x, count_x), pl.ds(to_y, count_y)],
            dx,
            dy,
        )

    finished(copies_of(4, [coarsest_piece(dx, dy) for dx, dy in WAYS]))

    c2a[...] = (-16.0 * weight) * r2[...]
    sweep(c2a, c2b, r2, 1, planes2 + 9, 0, 16.0)
    sweep(c2b, c2a, r2, 2, planes2 + 8, 0, 16.0)
    sweep(c2a, c2b, r2, 3, planes2 + 7, 0, 16.0)

    def prolong(coarse, count, tall, wide, table):
        half = tall.shape[1] // 2
        for m in range(count):
            value = coarse[m + 3, pl.ds(ROWS // 2, half), :]
            tall[m, pl.ds(0, half, stride=2), :] = value
            tall[m, pl.ds(1, half, stride=2), :] = value
        wide[...] = spread(
            tall[...].reshape(count * tall.shape[1], tall.shape[2]), table[...]
        ).reshape(wide.shape)

    def add_pair(fine, wide, m, first):
        value = wide[m]
        fine[first] = fine[first] + value
        fine[first + 1] = fine[first + 1] + value

    prolong(c2b, planes2 + 4, tall1, rise1, up_z1)
    loop(0, planes2 + 4, lambda m: add_pair(p1b, rise1, m, 2 * m + 1))
    sweep(p1b, p1a, r1, 2, planes1 + 8, 0, 4.0)
    sweep(p1a, p1b, r1, 3, planes1 + 7, 0, 4.0)

    prolong(p1b, planes1 + 4, tall0, rise0, up_z0)
    loop(0, planes1 + 4, lambda m: add_pair(pa, rise0, m, 2 * m + 2))
    sweep(pa, pb, src, 3, planes + 9, -1, 1.0)

    def last(i):
        total, mid = own_rows(pb, i, rows)
        total = total - src[i - 1, pl.ds(ROWS, rows), :]
        pa[i, pl.ds(ROWS, rows), :] = (1.0 - relax_weight) * mid + weight * total

    loop(4, planes + 8, last)

    def finish(k):
        inside = pl.ds(ROWS, rows)
        out[k, 0] = pa[k + 6, inside, :]
        ahead = pa[k + 7, inside, :] - pa[k + 5, inside, :]
        further = pa[k + 8, inside, :] - pa[k + 4, inside, :]
        out[k, 1] = (8.0 * ahead - further) * (1.0 / 12.0)

    loop(0, planes, finish)
    star_copy.wait()


def pairing(fine, coarse, wrap=0):
    coarse_at = np.arange(coarse)
    if wrap:
        coarse_at = coarse_at % wrap
    return (np.arange(fine)[:, None] // 2 == coarse_at[None, :]).astype(np.float32)


def two_parts(table):
    upper = table.astype(ml_dtypes.bfloat16)
    lower = (table - upper.astype(np.float32)).astype(ml_dtypes.bfloat16)
    return [jnp.asarray(upper), jnp.asarray(lower)]


def predict_and_cycle(velocity, obstacle, pressure, row_tables, depth_tables, sizes):
    planes, rows, depth = pressure.shape
    _, thick, height, _ = velocity.shape
    planes1, rows1, depth1 = planes // 2, rows // 2, depth // 2
    planes2, rows2, depth2 = planes // 4, rows // 4, depth // 4
    down_z0 = pairing(depth, depth1)
    down_z1 = pairing(depth1, depth1, depth2)
    up_z1 = pairing(depth1, depth1).T
    up_z0 = pairing(depth, depth1).T
    tables = two_parts(np.concatenate(row_tables, axis=0))
    tables += two_parts(np.concatenate([table.T for table in depth_tables], axis=1))
    before, after = stream_planes(velocity)
    across = transverse(velocity, tables)
    tables += [
        jnp.asarray(table, jnp.bfloat16) for table in (down_z0, down_z1, up_z1, up_z0)
    ]

    def vmem(*shape):
        return pltpu.VMEM(shape, jnp.float32)

    return pl.pallas_call(
        functools.partial(cycle_kernel, sizes),
        out_shape=(
            jax.ShapeDtypeStruct(velocity.shape, jnp.float32),
            jax.ShapeDtypeStruct((planes, 2, rows, depth), jnp.float32),
        ),
        in_specs=[pl.BlockSpec(memory_space=pl.ANY)] * 6
        + [pl.BlockSpec(memory_space=pltpu.VMEM)] * len(tables),
        out_specs=(
            pl.BlockSpec(memory_space=pl.ANY),
            pl.BlockSpec(memory_space=pltpu.VMEM),
        ),
        scratch_shapes=[
            vmem(3, thick, height, depth),
            pltpu.VMEM((thick, height, depth), jnp.int32),
            vmem(3, thick, height, depth),
            vmem(3, thick, height, depth),
            vmem(3, thick, height, depth),
            vmem(3, thick, height, depth),
            vmem(thick, height, depth),
            pltpu.VMEM((height, depth), jnp.bfloat16),
            pltpu.VMEM((height, depth), jnp.bfloat16),
            vmem(planes + 12, rows + 16, depth),
            vmem(planes + 12, rows + 16, depth),
            vmem(planes + 10, rows + 16, depth),
            vmem(planes + 4, rows, depth),
            vmem(planes1, rows, depth),
            vmem(planes1, rows, depth1),
            vmem(planes1 + 10, rows1 + 16, depth1),
            vmem(planes1 + 10, rows1 + 16, depth1),
            vmem(planes1 + 10, rows1 + 16, depth1),
            vmem(planes2 + 2, rows1, depth1),
            vmem(planes2 + 2, rows1, depth1),
            vmem(planes2 + 2, rows2, depth1),
            vmem(planes2 + 10, rows2 + 16, depth1),
            vmem(planes2 + 10, rows2 + 16, depth1),
            vmem(planes2 + 10, rows2 + 16, depth1),
            vmem(planes2 + 4, rows1 + 16, depth1),
            vmem(planes2 + 4, rows1 + 16, depth1),
            vmem(planes1 + 4, rows + 16, depth1),
            vmem(planes1 + 4, rows + 16, depth),
            pltpu.SemaphoreType.DMA((18,)),
            pltpu.SemaphoreType.DMA((9, 8)),
            pltpu.SemaphoreType.DMA((9, 8)),
        ],
        compiler_params=pltpu.CompilerParams(
            collective_id=1, has_side_effects=True, vmem_limit_bytes=56 * 2**20
        ),
        name="predict_and_cycle",
    )(velocity, before, after, across, obstacle, pressure, *tables)


def local(sizes, velocity, obstacle, pressure):
    row_tables = compact_tables(velocity.shape[2])
    depth_tables = compact_tables(velocity.shape[3])
    keep = 1.0 - obstacle.astype(jnp.float32)
    star, result = predict_and_cycle(
        velocity, obstacle, pressure, row_tables, depth_tables, sizes
    )
    thick, height, depth = obstacle.shape
    slabs = lax.all_to_all(result, "group", split_axis=0, concat_axis=0, tiled=True)
    slabs = slabs.reshape(sizes[1], thick, 2, height // sizes[1], depth)
    returned = slabs.transpose(2, 1, 0, 3, 4).reshape(2, thick, height, depth)
    gradient = jnp.stack(
        [
            returned[1],
            along_rows(row_tables[0], returned[0]),
            along_depth(depth_tables[0], returned[0]),
        ]
    )
    corrected = (star - gradient) * keep
    return (corrected, result[:, 0])


def solution(mesh):
    in_specs = (
        P(None, ("tunnel", "group"), None, None),
        P(("tunnel", "group"), None, None),
        P("tunnel", "group", None),
    )
    out_specs = (P(None, ("tunnel", "group"), None, None), P("tunnel", "group", None))
    sizes = (mesh.shape["tunnel"], mesh.shape["group"])
    return jax.shard_map(
        functools.partial(local, sizes),
        mesh=mesh,
        in_specs=in_specs,
        out_specs=out_specs,
        check_vma=False,
    )
```

```python
import functools
import math

import jax
import jax.numpy as jnp
import ml_dtypes
import numpy as np
from jax import lax
from jax.experimental import pallas as pl
from jax.experimental.pallas import tpu as pltpu
from jax.sharding import PartitionSpec as P

time_step = 0.1
viscosity = 0.05
relax_weight = 0.8
high = lax.Precision.HIGH
MESH = pl.DeviceIdType.MESH

ROWS = 8
PLANES_P = 6
PLANES_S = 5
PLANES_1 = 5
PLANES_2 = 5
WAYS = [(dx, dy) for dx in (-1, 0, 1) for dy in (-1, 0, 1) if (dx, dy) != (0, 0)]


def compact_tables(count):
    indices = np.arange(count)
    angles = (indices[:, None] * indices[None, :] % count) * (2.0 * math.pi / count)
    cosines = np.cos(angles)
    sines = np.sin(angles)
    theta = indices * (2.0 * math.pi / count)
    first_wave = (14.0 / 9.0 * np.sin(theta) + np.sin(2.0 * theta) / 18.0) / (
        1.0 + 2.0 / 3.0 * np.cos(theta)
    )
    second_wave = (
        24.0 / 11.0 * (1.0 - np.cos(theta)) + 3.0 / 22.0 * (1.0 - np.cos(2.0 * theta))
    ) / (1.0 + 4.0 / 11.0 * np.cos(theta))
    first = ((cosines * first_wave) @ sines.T - (sines * first_wave) @ cosines.T) / count
    second = -((cosines * second_wave) @ cosines.T + (sines * second_wave) @ sines.T) / count
    return first.astype(np.float32), second.astype(np.float32)


def along_rows(matrix, field):
    return jnp.einsum("ij,...jz->...iz", matrix, field, precision=high)


def along_depth(matrix, field):
    return jnp.einsum("...j,ij->...i", field, matrix, precision=high)


def part(step, length, halo):
    if step > 0:
        return length - halo, halo, 0
    if step < 0:
        return 0, halo, halo + length
    return 0, length, halo


def neighbour(sizes, dx, dy):
    me_x = lax.axis_index("tunnel")
    me_y = lax.axis_index("group")
    return (
        lax.rem(me_x + (dx + sizes[0]), sizes[0]),
        lax.rem(me_y + (dy + sizes[1]), sizes[1]),
    )


def stream_planes(value):
    size = lax.axis_size(("tunnel", "group"))
    up = [(i, (i + 1) % size) for i in range(size)]
    down = [(j, i) for i, j in up]
    before = lax.ppermute(value, ("tunnel", "group"), up)
    after = lax.ppermute(value, ("tunnel", "group"), down)
    return before, after


def member(sizes, ahead):
    return lax.axis_index("tunnel"), lax.rem(lax.axis_index("group") + ahead, sizes[1])


def enter(sizes):
    barrier = pltpu.get_barrier_semaphore()
    partners = [neighbour(sizes, dx, dy) for dx, dy in WAYS]
    partners += [member(sizes, ahead) for ahead in range(1, sizes[1])]
    for partner in partners:
        pl.semaphore_signal(barrier, inc=1, device_id=partner, device_id_type=MESH)
    pl.semaphore_wait(barrier, len(partners))


def loop(start, stop, body, unroll=4):
    whole = (stop - start) // unroll

    def several(step, carry):
        for lane in range(unroll):
            body(start + step * unroll + lane)
        return carry

    if whole:
        lax.fori_loop(0, whole, several, 0)
    for index in range(start + whole * unroll, stop):
        body(index)


def around(value):
    rows, depth = value.shape
    total = pltpu.roll(value, 1, 0) + pltpu.roll(value, rows - 1, 0)
    return total + pltpu.roll(value, 1, 1) + pltpu.roll(value, depth - 1, 1)


def sweep(source, target, right, start, stop, offset, scale):
    weight = relax_weight / 6.0

    def body(i):
        mid = source[i]
        total = source[i + 1] + source[i - 1] + around(mid)
        if scale == 1.0:
            total = total - right[i + offset]
        else:
            total = total - scale * right[i + offset]
        target[i] = (1.0 - relax_weight) * mid + weight * total

    loop(start, stop, body)


def own_rows(source, i, rows):
    span = source[i]
    rolled = pltpu.roll(span, 1, 0) + pltpu.roll(span, rows + 2 * ROWS - 1, 0)
    inside = pl.ds(ROWS, rows)
    mid = source[i, inside, :]
    total = source[i + 1, inside, :] + source[i - 1, inside, :] + rolled[ROWS : ROWS + rows]
    depth = mid.shape[1]
    return total + pltpu.roll(mid, 1, 1) + pltpu.roll(mid, depth - 1, 1), mid


def leftover(source, right, i, offset, scale, rows):
    total, mid = own_rows(source, i, rows)
    return right[i + offset, pl.ds(ROWS, rows), :] - (total - 6.0 * mid) * (1.0 / scale)


def spread(value, table):
    upper = value.astype(jnp.bfloat16)
    lower = (value - upper.astype(jnp.float32)).astype(jnp.bfloat16)
    return jnp.dot(upper, table, preferred_element_type=jnp.float32) + jnp.dot(
        lower, table, preferred_element_type=jnp.float32
    )


def halves(value):
    upper = value.astype(jnp.bfloat16)
    return upper, (value - upper.astype(jnp.float32)).astype(jnp.bfloat16)


def product(a, b):
    return jnp.dot(a, b, preferred_element_type=jnp.float32)


def transverse_kernel(vel, rows_high, rows_low, depth_high, depth_low, base, high, low):
    height, depth = vel.shape[2], vel.shape[3]
    first, second = pl.ds(0, height), pl.ds(height, height)

    def component(c, carry):
        upper, lower = halves(vel[c, 0])
        high[...] = upper
        low[...] = lower
        row_first = (
            product(rows_high[first, :], high[...])
            + product(rows_high[first, :], low[...])
            + product(rows_low[first, :], high[...])
        )
        row_second = (
            product(rows_high[second, :], high[...])
            + product(rows_high[second, :], low[...])
            + product(rows_low[second, :], high[...])
        )
        along = (
            product(high[...], depth_high[...])
            + product(low[...], depth_high[...])
            + product(high[...], depth_low[...])
        )
        advection = vel[1, 0] * row_first + vel[2, 0] * along[:, :depth]
        base[c, 0] = vel[c, 0] + time_step * (
            viscosity * (row_second + along[:, depth:]) - advection
        )
        return carry

    lax.fori_loop(0, 3, component, 0)


def transverse(velocity, tables):
    _, thick, height, depth = velocity.shape
    plane = pl.BlockSpec((3, 1, height, depth), lambda p: (0, p, 0, 0))
    flops = 2 * 9 * thick * height * depth * 2 * (height + depth)
    return pl.pallas_call(
        transverse_kernel,
        grid=(thick,),
        out_shape=jax.ShapeDtypeStruct(velocity.shape, jnp.float32),
        in_specs=[plane] + [pl.BlockSpec(memory_space=pltpu.VMEM)] * 4,
        out_specs=plane,
        scratch_shapes=[pltpu.VMEM((height, depth), jnp.bfloat16)] * 2,
        compiler_params=pltpu.CompilerParams(vmem_limit_bytes=32 * 2**20),
        cost_estimate=pl.CostEstimate(
            flops=flops, bytes_accessed=8 * 3 * thick * height * depth, transcendentals=0
        ),
        name="transverse",
    )(velocity, *tables)


def cycle_kernel(
    sizes,
    velocity,
    before,
    after,
    across,
    obstacle,
    pressure,
    rows_high,
    rows_low,
    depth_high,
    depth_low,
    down_z0,
    down_z1,
    up_z1,
    up_z0,
    star_out,
    potential_out,
    out,
    vel,
    leaf,
    solid,
    left,
    right,
    base,
    stars,
    cross,
    high,
    low,
    pa,
    pb,
    src,
    star,
    fine0,
    half0,
    r1,
    p1a,
    p1b,
    fine1,
    half1,
    r2s,
    r2,
    c2a,
    c2b,
    tall1,
    rise1,
    tall0,
    rise0,
    local_sem,
    send_sem,
    recv_sem,
):
    planes, rows, depth = pressure.shape
    planes1, rows1, depth1 = planes // 2, rows // 2, depth // 2
    planes2, rows2 = planes // 4, rows // 4
    weight = relax_weight / 6.0
    near, far = 2, PLANES_S - 2
    thick, height = velocity.shape[1], velocity.shape[2]
    members = sizes[1]
    me_y = lax.axis_index("group")

    def copy_to(group, way, source, target, device):
        copy = pltpu.make_async_remote_copy(
            src_ref=source,
            dst_ref=target,
            send_sem=send_sem.at[group, way],
            recv_sem=recv_sem.at[group, way],
            device_id=device,
            device_id_type=MESH,
        )
        copy.start()
        return copy

    def copies_of(group, pieces):
        return [
            copy_to(group, way, source, target, neighbour(sizes, dx, dy))
            for way, (source, target, dx, dy) in enumerate(pieces)
        ]

    def finished(copies):
        for copy in copies:
            copy.wait()

    def here(source, target, index):
        copy = pltpu.make_async_copy(source, target, local_sem.at[index])
        copy.start()
        return copy

    def load(c):
        pairs = [(velocity, vel), (before, left), (after, right), (across, base)]
        return [
            here(source.at[c], target.at[c], 6 + 4 * c + index)
            for index, (source, target) in enumerate(pairs)
        ]

    loads = [load(0)]
    own_solid = here(obstacle, solid, 1)
    loads += [load(1), load(2)]
    own_pressure = here(pressure, pa.at[pl.ds(PLANES_P, planes), pl.ds(ROWS, rows)], 2)
    enter(sizes)

    near_pressure = PLANES_P // 2

    def pressure_piece(dx, dy, shift, count):
        if dx > 0:
            from_x, to_x = planes - shift - count, PLANES_P - shift - count
        elif dx < 0:
            from_x, to_x = shift, PLANES_P + planes + shift
        else:
            from_x, to_x, count = 0, PLANES_P, planes
        from_y, count_y, to_y = part(dy, rows, ROWS)
        return (
            pressure.at[pl.ds(from_x, count), pl.ds(from_y, count_y)],
            pa.at[pl.ds(to_x, count), pl.ds(to_y, count_y)],
            dx,
            dy,
        )

    pressure_copies = copies_of(
        5, [pressure_piece(dx, dy, 0, near_pressure) for dx, dy in WAYS]
    )

    def block(index):
        return pl.ds(pl.multiple_of(index * rows, rows), rows)

    def predict(c, at):
        near_planes = [left.at[c, 0], left.at[c, 1], vel.at[c, 0], vel.at[c, 1]]
        near_planes += [right.at[c, 0], right.at[c, 1]]
        f = [plane[at, :] for plane in near_planes]
        for p in range(thick):
            ahead, further = f[p + 3] - f[p + 1], f[p + 4] - f[p]
            slope = (8.0 * ahead - further) * (1.0 / 12.0)
            beside, beyond = f[p + 3] + f[p + 1], f[p + 4] + f[p]
            bend = (16.0 * beside - beyond - 30.0 * f[p + 2]) * (1.0 / 12.0)
            keep = 1.0 - solid[p, at, :].astype(jnp.float32)
            stars[c, p, at, :] = keep * (
                base[c, p, at, :]
                + time_step * (viscosity * bend - vel[0, p, at, :] * slope)
            )

    def slabs(group, make, source, target):
        copies = []
        for ahead in range(1, members):
            device = member(sizes, ahead)
            at = block(device[1])
            make(at)
            copies.append(copy_to(group, ahead - 1, source(at), target, device))
        make(block(me_y))
        return copies

    mine = block(me_y)

    finished(loads[0])
    own_solid.wait()
    star_at = star.at[pl.ds(2 + me_y * thick, thick)]
    star_slabs = slabs(
        7, lambda at: predict(0, at), lambda at: stars.at[0, :, at, :], star_at
    )
    own_star = here(stars.at[0, :, mine, :], star_at, 3)

    finished(loads[1])
    loop(0, members, lambda k: predict(1, block(k)), 2)
    for p in range(thick):
        upper, lower = halves(stars[1, p])
        high[...] = upper
        low[...] = lower
        first = pl.ds(0, height)
        cross[p] = (
            product(rows_high[first, :], high[...])
            + product(rows_high[first, :], low[...])
            + product(rows_low[first, :], high[...])
        )

    finished(loads[2])

    def diverge(at):
        predict(2, at)
        wave_high, wave_low = depth_high[:, pl.ds(0, depth)], depth_low[:, pl.ds(0, depth)]
        upper, lower = halves(stars[2, :, at, :].reshape(thick * rows, depth))
        along = product(upper, wave_high) + product(lower, wave_high) + product(upper, wave_low)
        for p in range(thick):
            cross[p, at, :] = cross[p, at, :] + along[p * rows : (p + 1) * rows]

    src_at = src.at[pl.ds(PLANES_S + me_y * thick, thick), pl.ds(ROWS, rows)]
    src_slabs = slabs(8, diverge, lambda at: cross.at[:, at, :], src_at)
    own_src = here(cross.at[:, mine, :], src_at, 4)
    star_copy = here(stars, star_out, 5)
    own_star.wait()
    finished(star_slabs)
    star_copies = copies_of(
        0,
        [
            (star.at[pl.ds(planes, 2)], star.at[pl.ds(0, 2)], 1, 0),
            (star.at[pl.ds(2, 2)], star.at[pl.ds(planes + 2, 2)], -1, 0),
        ],
    )

    finished(star_copies)
    own_src.wait()
    finished(src_slabs)

    def divergence(k):
        inside = pl.ds(ROWS, rows)
        ahead = star[k + 3] - star[k + 1]
        further = star[k + 4] - star[k]
        src[k + PLANES_S, inside, :] = src[k + PLANES_S, inside, :] + (
            8.0 * ahead - further
        ) * (1.0 / 12.0)

    loop(0, planes, divergence)

    def source_piece(dx, dy, shift, count):
        if dx > 0:
            from_x, to_x = PLANES_S + planes - shift - count, PLANES_S - shift - count
        elif dx < 0:
            from_x, to_x = PLANES_S + shift, PLANES_S + planes + shift
        else:
            from_x, to_x, count = PLANES_S, PLANES_S, planes
        from_y, count_y, to_y = part(dy, rows, ROWS)
        return (
            src.at[pl.ds(from_x, count), pl.ds(ROWS + from_y, count_y)],
            src.at[pl.ds(to_x, count), pl.ds(to_y, count_y)],
            dx,
            dy,
        )

    near_copies = copies_of(1, [source_piece(dx, dy, 0, near) for dx, dy in WAYS])
    own_pressure.wait()
    finished(pressure_copies)
    finished(near_copies)

    sweep(pa, pb, src, 4, planes + 8, -1, 1.0)
    sweep(pb, pa, src, 5, planes + 7, -1, 1.0)

    def restrict0(m):
        fine0[m] = leftover(pa, src, 2 * m + 6, -1, 1.0, rows) + leftover(
            pa, src, 2 * m + 7, -1, 1.0, rows
        )

    loop(0, planes1, restrict0, 2)
    half0[...] = spread(
        fine0[...].reshape(planes1 * rows, depth), down_z0[...]
    ).reshape(planes1, rows, depth1)
    for m in range(planes1):
        r1[m + PLANES_1, pl.ds(ROWS, rows1), :] = 0.125 * (
            half0[m, pl.ds(0, rows1, stride=2), :] + half0[m, pl.ds(1, rows1, stride=2), :]
        )

    def residual_piece(dx, dy):
        from_x, count_x, to_x = part(dx, planes1, PLANES_1)
        from_y, count_y, to_y = part(dy, rows1, ROWS)
        return (
            r1.at[pl.ds(PLANES_1 + from_x, count_x), pl.ds(ROWS + from_y, count_y)],
            r1.at[pl.ds(to_x, count_x), pl.ds(to_y, count_y)],
            dx,
            dy,
        )

    coarse_copies = copies_of(3, [residual_piece(dx, dy) for dx, dy in WAYS])

    sideways = [(dx, dy) for dx, dy in WAYS if dx]
    far_copies = copies_of(2, [source_piece(dx, dy, near, far) for dx, dy in sideways])
    far_copies += copies_of(
        9,
        [
            pressure_piece(dx, dy, near_pressure, PLANES_P - near_pressure)
            for dx, dy in sideways
        ],
    )
    finished(coarse_copies)

    p1a[...] = (-4.0 * weight) * r1[...]
    sweep(p1a, p1b, r1, 1, planes1 + 9, 0, 4.0)

    def restrict1(m):
        fine1[m] = leftover(p1b, r1, 2 * m + 3, 0, 4.0, rows1) + leftover(
            p1b, r1, 2 * m + 4, 0, 4.0, rows1
        )

    loop(0, planes2 + 2, restrict1, 2)
    half1[...] = spread(
        fine1[...].reshape((planes2 + 2) * rows1, depth1), down_z1[...]
    ).reshape(planes2 + 2, rows1, depth1)
    for m in range(planes2 + 2):
        value = 0.125 * (
            half1[m, pl.ds(0, rows2, stride=2), :] + half1[m, pl.ds(1, rows2, stride=2), :]
        )
        r2s[m] = value
        if 0 < m <= planes2:
            r2[m + PLANES_2 - 1, pl.ds(ROWS, rows2), :] = value

    def coarsest_piece(dx, dy):
        from_x, count_x, to_x = {
            1: (0, PLANES_2, 0),
            -1: (1, PLANES_2, PLANES_2 + planes2),
            0: (1, planes2, PLANES_2),
        }[dx]
        from_y, count_y, to_y = part(dy, rows2, ROWS)
        return (
            r2s.at[pl.ds(from_x, count_x), pl.ds(from_y, count_y)],
            r2.at[pl.ds(to_x, count_x), pl.ds(to_y, count_y)],
            dx,
            dy,
        )

    coarsest_copies = copies_of(4, [coarsest_piece(dx, dy) for dx, dy in WAYS])

    finished(far_copies)
    sweep(pa, pb, src, 1, 4, -1, 1.0)
    sweep(pa, pb, src, planes + 8, planes + 11, -1, 1.0)
    sweep(pb, pa, src, 2, 5, -1, 1.0)
    sweep(pb, pa, src, planes + 7, planes + 10, -1, 1.0)
    finished(coarsest_copies)

    c2a[...] = (-16.0 * weight) * r2[...]
    sweep(c2a, c2b, r2, 1, planes2 + 9, 0, 16.0)
    sweep(c2b, c2a, r2, 2, planes2 + 8, 0, 16.0)
    sweep(c2a, c2b, r2, 3, planes2 + 7, 0, 16.0)

    def prolong(coarse, count, tall, wide, table):
        half = tall.shape[1] // 2
        for m in range(count):
            value = coarse[m + 3, pl.ds(ROWS // 2, half), :]
            tall[m, pl.ds(0, half, stride=2), :] = value
            tall[m, pl.ds(1, half, stride=2), :] = value
        wide[...] = spread(
            tall[...].reshape(count * tall.shape[1], tall.shape[2]), table[...]
        ).reshape(wide.shape)

    def add_pair(fine, wide, m, first):
        value = wide[m]
        fine[first] = fine[first] + value
        fine[first + 1] = fine[first + 1] + value

    prolong(c2b, planes2 + 4, tall1, rise1, up_z1)
    loop(0, planes2 + 4, lambda m: add_pair(p1b, rise1, m, 2 * m + 1))
    sweep(p1b, p1a, r1, 2, planes1 + 8, 0, 4.0)
    sweep(p1a, p1b, r1, 3, planes1 + 7, 0, 4.0)

    prolong(p1b, planes1 + 4, tall0, rise0, up_z0)
    loop(0, planes1 + 4, lambda m: add_pair(pa, rise0, m, 2 * m + 2))
    sweep(pa, pb, src, 3, planes + 9, -1, 1.0)

    def last(i):
        total, mid = own_rows(pb, i, rows)
        total = total - src[i - 1, pl.ds(ROWS, rows), :]
        pa[i, pl.ds(ROWS, rows), :] = (1.0 - relax_weight) * mid + weight * total

    loop(4, planes + 8, last)

    tile = pl.ds(ROWS, rows)
    potential_copy = here(pa.at[pl.ds(PLANES_P, planes), tile], potential_out, 0)

    def own_planes(index):
        return pl.ds(PLANES_P + index * thick, thick)

    back_at = out.at[0, :, mine, :]
    back = []
    for ahead in range(1, members):
        device = member(sizes, ahead)
        back.append(
            copy_to(10, ahead - 1, pa.at[own_planes(device[1]), tile], back_at, device)
        )
    own_back = here(pa.at[own_planes(me_y), tile], back_at, 1)

    def slope_of(k):
        ahead = pa[k + 7, tile, :] - pa[k + 5, tile, :]
        further = pa[k + 8, tile, :] - pa[k + 4, tile, :]
        leaf[k] = (8.0 * ahead - further) * (1.0 / 12.0)

    slope_at = out.at[1, :, mine, :]
    for ahead in range(1, members + 1):
        device = member(sizes, ahead)
        for p in range(thick):
            slope_of(device[1] * thick + p)
        source = leaf.at[pl.ds(device[1] * thick, thick)]
        if ahead < members:
            back.append(copy_to(11, ahead - 1, source, slope_at, device))
        else:
            own_slope = here(source, slope_at, 2)
    potential_copy.wait()
    own_back.wait()
    own_slope.wait()
    finished(back)
    star_copy.wait()


def pairing(fine, coarse, wrap=0):
    coarse_at = np.arange(coarse)
    if wrap:
        coarse_at = coarse_at % wrap
    return (np.arange(fine)[:, None] // 2 == coarse_at[None, :]).astype(np.float32)


def two_parts(table):
    upper = table.astype(ml_dtypes.bfloat16)
    lower = (table - upper.astype(np.float32)).astype(ml_dtypes.bfloat16)
    return [jnp.asarray(upper), jnp.asarray(lower)]


def predict_and_cycle(velocity, obstacle, pressure, row_tables, depth_tables, sizes):
    planes, rows, depth = pressure.shape
    _, thick, height, _ = velocity.shape
    planes1, rows1, depth1 = planes // 2, rows // 2, depth // 2
    planes2, rows2, depth2 = planes // 4, rows // 4, depth // 4
    down_z0 = pairing(depth, depth1)
    down_z1 = pairing(depth1, depth1, depth2)
    up_z1 = pairing(depth1, depth1).T
    up_z0 = pairing(depth, depth1).T
    tables = two_parts(np.concatenate(row_tables, axis=0))
    tables += two_parts(np.concatenate([table.T for table in depth_tables], axis=1))
    before, after = stream_planes(velocity)
    across = transverse(velocity, tables)
    tables += [
        jnp.asarray(table, jnp.bfloat16) for table in (down_z0, down_z1, up_z1, up_z0)
    ]

    def vmem(*shape):
        return pltpu.VMEM(shape, jnp.float32)

    return pl.pallas_call(
        functools.partial(cycle_kernel, sizes),
        out_shape=(
            jax.ShapeDtypeStruct(velocity.shape, jnp.float32),
            jax.ShapeDtypeStruct(pressure.shape, jnp.float32),
            jax.ShapeDtypeStruct((2, thick, height, depth), jnp.float32),
        ),
        in_specs=[pl.BlockSpec(memory_space=pl.ANY)] * 6
        + [pl.BlockSpec(memory_space=pltpu.VMEM)] * len(tables),
        out_specs=(
            pl.BlockSpec(memory_space=pl.ANY),
            pl.BlockSpec(memory_space=pl.ANY),
            pl.BlockSpec(memory_space=pltpu.VMEM),
        ),
        scratch_shapes=[
            vmem(3, thick, height, depth),
            vmem(planes, rows, depth),
            pltpu.VMEM((thick, height, depth), jnp.int32),
            vmem(3, thick, height, depth),
            vmem(3, thick, height, depth),
            vmem(3, thick, height, depth),
            vmem(3, thick, height, depth),
            vmem(thick, height, depth),
            pltpu.VMEM((height, depth), jnp.bfloat16),
            pltpu.VMEM((height, depth), jnp.bfloat16),
            vmem(planes + 12, rows + 16, depth),
            vmem(planes + 12, rows + 16, depth),
            vmem(planes + 10, rows + 16, depth),
            vmem(planes + 4, rows, depth),
            vmem(planes1, rows, depth),
            vmem(planes1, rows, depth1),
            vmem(planes1 + 10, rows1 + 16, depth1),
            vmem(planes1 + 10, rows1 + 16, depth1),
            vmem(planes1 + 10, rows1 + 16, depth1),
            vmem(planes2 + 2, rows1, depth1),
            vmem(planes2 + 2, rows1, depth1),
            vmem(planes2 + 2, rows2, depth1),
            vmem(planes2 + 10, rows2 + 16, depth1),
            vmem(planes2 + 10, rows2 + 16, depth1),
            vmem(planes2 + 10, rows2 + 16, depth1),
            vmem(planes2 + 4, rows1 + 16, depth1),
            vmem(planes2 + 4, rows1 + 16, depth1),
            vmem(planes1 + 4, rows + 16, depth1),
            vmem(planes1 + 4, rows + 16, depth),
            pltpu.SemaphoreType.DMA((18,)),
            pltpu.SemaphoreType.DMA((12, 8)),
            pltpu.SemaphoreType.DMA((12, 8)),
        ],
        compiler_params=pltpu.CompilerParams(
            collective_id=1, has_side_effects=True, vmem_limit_bytes=56 * 2**20
        ),
        name="predict_and_cycle",
    )(velocity, before, after, across, obstacle, pressure, *tables)


def local(sizes, velocity, obstacle, pressure):
    row_tables = compact_tables(velocity.shape[2])
    depth_tables = compact_tables(velocity.shape[3])
    keep = 1.0 - obstacle.astype(jnp.float32)
    star, potential, returned = predict_and_cycle(
        velocity, obstacle, pressure, row_tables, depth_tables, sizes
    )
    gradient = jnp.stack(
        [
            returned[1],
            along_rows(row_tables[0], returned[0]),
            along_depth(depth_tables[0], returned[0]),
        ]
    )
    corrected = (star - gradient) * keep
    return (corrected, potential)


def solution(mesh):
    in_specs = (
        P(None, ("tunnel", "group"), None, None),
        P(("tunnel", "group"), None, None),
        P("tunnel", "group", None),
    )
    out_specs = (P(None, ("tunnel", "group"), None, None), P("tunnel", "group", None))
    sizes = (mesh.shape["tunnel"], mesh.shape["group"])
    return jax.shard_map(
        functools.partial(local, sizes),
        mesh=mesh,
        in_specs=in_specs,
        out_specs=out_specs,
        check_vma=False,
    )
```

```python
import functools
import math

import jax
import jax.numpy as jnp
import ml_dtypes
import numpy as np
from jax import lax
from jax.experimental import pallas as pl
from jax.experimental.pallas import tpu as pltpu
from jax.sharding import PartitionSpec as P

time_step = 0.1
viscosity = 0.05
relax_weight = 0.8
high = lax.Precision.HIGH
MESH = pl.DeviceIdType.MESH

ROWS = 8
PLANES_P = 6
PLANES_S = 5
PLANES_1 = 5
PLANES_2 = 5
WAYS = [(dx, dy) for dx in (-1, 0, 1) for dy in (-1, 0, 1) if (dx, dy) != (0, 0)]


def compact_tables(count):
    indices = np.arange(count)
    angles = (indices[:, None] * indices[None, :] % count) * (2.0 * math.pi / count)
    cosines = np.cos(angles)
    sines = np.sin(angles)
    theta = indices * (2.0 * math.pi / count)
    first_wave = (14.0 / 9.0 * np.sin(theta) + np.sin(2.0 * theta) / 18.0) / (
        1.0 + 2.0 / 3.0 * np.cos(theta)
    )
    second_wave = (
        24.0 / 11.0 * (1.0 - np.cos(theta)) + 3.0 / 22.0 * (1.0 - np.cos(2.0 * theta))
    ) / (1.0 + 4.0 / 11.0 * np.cos(theta))
    first = ((cosines * first_wave) @ sines.T - (sines * first_wave) @ cosines.T) / count
    second = -((cosines * second_wave) @ cosines.T + (sines * second_wave) @ sines.T) / count
    return first.astype(np.float32), second.astype(np.float32)


def along_rows(matrix, field):
    return jnp.einsum("ij,...jz->...iz", matrix, field, precision=high)


def along_depth(matrix, field):
    return jnp.einsum("...j,ij->...i", field, matrix, precision=high)


def part(step, length, halo):
    if step > 0:
        return length - halo, halo, 0
    if step < 0:
        return 0, halo, halo + length
    return 0, length, halo


def neighbour(sizes, dx, dy):
    me_x = lax.axis_index("tunnel")
    me_y = lax.axis_index("group")
    return (
        lax.rem(me_x + (dx + sizes[0]), sizes[0]),
        lax.rem(me_y + (dy + sizes[1]), sizes[1]),
    )


def stream_planes(value):
    size = lax.axis_size(("tunnel", "group"))
    up = [(i, (i + 1) % size) for i in range(size)]
    down = [(j, i) for i, j in up]
    before = lax.ppermute(value, ("tunnel", "group"), up)
    after = lax.ppermute(value, ("tunnel", "group"), down)
    return before, after


def member(sizes, ahead):
    return lax.axis_index("tunnel"), lax.rem(lax.axis_index("group") + ahead, sizes[1])


def enter(sizes):
    barrier = pltpu.get_barrier_semaphore()
    partners = [neighbour(sizes, dx, dy) for dx, dy in WAYS]
    partners += [member(sizes, ahead) for ahead in range(1, sizes[1])]
    for partner in partners:
        pl.semaphore_signal(barrier, inc=1, device_id=partner, device_id_type=MESH)
    pl.semaphore_wait(barrier, len(partners))


def loop(start, stop, body, unroll=4):
    whole = (stop - start) // unroll

    def several(step, carry):
        for lane in range(unroll):
            body(start + step * unroll + lane)
        return carry

    if whole:
        lax.fori_loop(0, whole, several, 0)
    for index in range(start + whole * unroll, stop):
        body(index)


def around(value):
    rows, depth = value.shape
    total = pltpu.roll(value, 1, 0) + pltpu.roll(value, rows - 1, 0)
    return total + pltpu.roll(value, 1, 1) + pltpu.roll(value, depth - 1, 1)


def sweep(source, target, right, start, stop, offset, scale):
    weight = relax_weight / 6.0

    def body(i):
        mid = source[i]
        total = source[i + 1] + source[i - 1] + around(mid)
        if scale == 1.0:
            total = total - right[i + offset]
        else:
            total = total - scale * right[i + offset]
        target[i] = (1.0 - relax_weight) * mid + weight * total

    loop(start, stop, body)


def own_rows(source, i, rows):
    span = source[i]
    rolled = pltpu.roll(span, 1, 0) + pltpu.roll(span, rows + 2 * ROWS - 1, 0)
    inside = pl.ds(ROWS, rows)
    mid = source[i, inside, :]
    total = source[i + 1, inside, :] + source[i - 1, inside, :] + rolled[ROWS : ROWS + rows]
    depth = mid.shape[1]
    return total + pltpu.roll(mid, 1, 1) + pltpu.roll(mid, depth - 1, 1), mid


def leftover(source, right, i, offset, scale, rows):
    total, mid = own_rows(source, i, rows)
    return right[i + offset, pl.ds(ROWS, rows), :] - (total - 6.0 * mid) * (1.0 / scale)


def spread(value, table):
    upper = value.astype(jnp.bfloat16)
    lower = (value - upper.astype(jnp.float32)).astype(jnp.bfloat16)
    return jnp.dot(upper, table, preferred_element_type=jnp.float32) + jnp.dot(
        lower, table, preferred_element_type=jnp.float32
    )


def halves(value):
    upper = value.astype(jnp.bfloat16)
    return upper, (value - upper.astype(jnp.float32)).astype(jnp.bfloat16)


def product(a, b):
    return jnp.dot(a, b, preferred_element_type=jnp.float32)


def transverse_kernel(vel, rows_high, rows_low, depth_high, depth_low, base, high, low):
    height, depth = vel.shape[2], vel.shape[3]
    first, second = pl.ds(0, height), pl.ds(height, height)

    def component(c, carry):
        upper, lower = halves(vel[c, 0])
        high[...] = upper
        low[...] = lower
        row_first = (
            product(rows_high[first, :], high[...])
            + product(rows_high[first, :], low[...])
            + product(rows_low[first, :], high[...])
        )
        row_second = (
            product(rows_high[second, :], high[...])
            + product(rows_high[second, :], low[...])
            + product(rows_low[second, :], high[...])
        )
        along = (
            product(high[...], depth_high[...])
            + product(low[...], depth_high[...])
            + product(high[...], depth_low[...])
        )
        advection = vel[1, 0] * row_first + vel[2, 0] * along[:, :depth]
        base[c, 0] = vel[c, 0] + time_step * (
            viscosity * (row_second + along[:, depth:]) - advection
        )
        return carry

    lax.fori_loop(0, 3, component, 0)


def transverse(velocity, tables):
    _, thick, height, depth = velocity.shape
    plane = pl.BlockSpec((3, 1, height, depth), lambda p: (0, p, 0, 0))
    flops = 2 * 9 * thick * height * depth * 2 * (height + depth)
    return pl.pallas_call(
        transverse_kernel,
        grid=(thick,),
        out_shape=jax.ShapeDtypeStruct(velocity.shape, jnp.float32),
        in_specs=[plane] + [pl.BlockSpec(memory_space=pltpu.VMEM)] * 4,
        out_specs=plane,
        scratch_shapes=[pltpu.VMEM((height, depth), jnp.bfloat16)] * 2,
        compiler_params=pltpu.CompilerParams(vmem_limit_bytes=32 * 2**20),
        cost_estimate=pl.CostEstimate(
            flops=flops, bytes_accessed=8 * 3 * thick * height * depth, transcendentals=0
        ),
        name="transverse",
    )(velocity, *tables)


def cycle_kernel(
    sizes,
    velocity,
    before,
    after,
    across,
    obstacle,
    pressure,
    rows_high,
    rows_low,
    depth_high,
    depth_low,
    down_z0,
    down_z1,
    up_z1,
    up_z0,
    star_out,
    potential_out,
    out,
    vel,
    leaf,
    solid,
    left,
    right,
    base,
    stars,
    cross,
    high,
    low,
    pa,
    pb,
    src,
    star,
    fine0,
    half0,
    r1,
    p1a,
    p1b,
    fine1,
    half1,
    r2s,
    r2,
    c2a,
    c2b,
    tall1,
    rise1,
    tall0,
    rise0,
    local_sem,
    send_sem,
    recv_sem,
):
    planes, rows, depth = pressure.shape
    planes1, rows1, depth1 = planes // 2, rows // 2, depth // 2
    planes2, rows2 = planes // 4, rows // 4
    weight = relax_weight / 6.0
    near, far = 2, PLANES_S - 2
    thick, height = velocity.shape[1], velocity.shape[2]
    members = sizes[1]
    me_y = lax.axis_index("group")

    def copy_to(group, way, source, target, device):
        copy = pltpu.make_async_remote_copy(
            src_ref=source,
            dst_ref=target,
            send_sem=send_sem.at[group, way],
            recv_sem=recv_sem.at[group, way],
            device_id=device,
            device_id_type=MESH,
        )
        copy.start()
        return copy

    def copies_of(group, pieces):
        return [
            copy_to(group, way, source, target, neighbour(sizes, dx, dy))
            for way, (source, target, dx, dy) in enumerate(pieces)
        ]

    def finished(copies):
        for copy in copies:
            copy.wait()

    def here(source, target, index):
        copy = pltpu.make_async_copy(source, target, local_sem.at[index])
        copy.start()
        return copy

    def load(c):
        pairs = [(velocity, vel), (before, left), (after, right), (across, base)]
        return [
            here(source.at[c], target.at[c], 6 + 4 * c + index)
            for index, (source, target) in enumerate(pairs)
        ]

    loads = [load(0)]
    own_solid = here(obstacle, solid, 1)
    loads += [load(1), load(2)]
    own_pressure = here(pressure, pa.at[pl.ds(PLANES_P, planes), pl.ds(ROWS, rows)], 2)
    enter(sizes)

    near_pressure = PLANES_P // 2

    def pressure_piece(dx, dy, shift, count):
        if dx > 0:
            from_x, to_x = planes - shift - count, PLANES_P - shift - count
        elif dx < 0:
            from_x, to_x = shift, PLANES_P + planes + shift
        else:
            from_x, to_x, count = 0, PLANES_P, planes
        from_y, count_y, to_y = part(dy, rows, ROWS)
        return (
            pressure.at[pl.ds(from_x, count), pl.ds(from_y, count_y)],
            pa.at[pl.ds(to_x, count), pl.ds(to_y, count_y)],
            dx,
            dy,
        )

    pressure_copies = copies_of(
        5, [pressure_piece(dx, dy, 0, near_pressure) for dx, dy in WAYS]
    )

    def block(index):
        return pl.ds(pl.multiple_of(index * rows, rows), rows)

    def predict(c, at):
        near_planes = [left.at[c, 0], left.at[c, 1], vel.at[c, 0], vel.at[c, 1]]
        near_planes += [right.at[c, 0], right.at[c, 1]]
        f = [plane[at, :] for plane in near_planes]
        for p in range(thick):
            ahead, further = f[p + 3] - f[p + 1], f[p + 4] - f[p]
            slope = (8.0 * ahead - further) * (1.0 / 12.0)
            beside, beyond = f[p + 3] + f[p + 1], f[p + 4] + f[p]
            bend = (16.0 * beside - beyond - 30.0 * f[p + 2]) * (1.0 / 12.0)
            keep = 1.0 - solid[p, at, :].astype(jnp.float32)
            stars[c, p, at, :] = keep * (
                base[c, p, at, :]
                + time_step * (viscosity * bend - vel[0, p, at, :] * slope)
            )

    def slabs(group, make, source, target):
        copies = []
        for ahead in range(1, members):
            device = member(sizes, ahead)
            at = block(device[1])
            make(at)
            copies.append(copy_to(group, ahead - 1, source(at), target, device))
        make(block(me_y))
        return copies

    mine = block(me_y)

    finished(loads[0])
    own_solid.wait()
    star_at = star.at[pl.ds(2 + me_y * thick, thick)]
    star_slabs = slabs(
        7, lambda at: predict(0, at), lambda at: stars.at[0, :, at, :], star_at
    )
    own_star = here(stars.at[0, :, mine, :], star_at, 3)

    finished(loads[1])
    loop(0, members, lambda k: predict(1, block(k)), 2)
    for p in range(thick):
        upper, lower = halves(stars[1, p])
        high[...] = upper
        low[...] = lower
        first = pl.ds(0, height)
        cross[p] = (
            product(rows_high[first, :], high[...])
            + product(rows_high[first, :], low[...])
            + product(rows_low[first, :], high[...])
        )

    finished(loads[2])

    def diverge(at):
        predict(2, at)
        wave_high, wave_low = depth_high[:, pl.ds(0, depth)], depth_low[:, pl.ds(0, depth)]
        upper, lower = halves(stars[2, :, at, :].reshape(thick * rows, depth))
        along = product(upper, wave_high) + product(lower, wave_high) + product(upper, wave_low)
        for p in range(thick):
            cross[p, at, :] = cross[p, at, :] + along[p * rows : (p + 1) * rows]

    src_at = src.at[pl.ds(PLANES_S + me_y * thick, thick), pl.ds(ROWS, rows)]
    src_slabs = slabs(8, diverge, lambda at: cross.at[:, at, :], src_at)
    own_src = here(cross.at[:, mine, :], src_at, 4)
    star_copy = here(stars, star_out, 5)
    own_star.wait()
    finished(star_slabs)
    star_copies = copies_of(
        0,
        [
            (star.at[pl.ds(planes, 2)], star.at[pl.ds(0, 2)], 1, 0),
            (star.at[pl.ds(2, 2)], star.at[pl.ds(planes + 2, 2)], -1, 0),
        ],
    )

    finished(star_copies)
    own_src.wait()
    finished(src_slabs)

    def divergence(k):
        inside = pl.ds(ROWS, rows)
        ahead = star[k + 3] - star[k + 1]
        further = star[k + 4] - star[k]
        src[k + PLANES_S, inside, :] = src[k + PLANES_S, inside, :] + (
            8.0 * ahead - further
        ) * (1.0 / 12.0)

    loop(0, planes, divergence)

    def source_piece(dx, dy, shift, count):
        if dx > 0:
            from_x, to_x = PLANES_S + planes - shift - count, PLANES_S - shift - count
        elif dx < 0:
            from_x, to_x = PLANES_S + shift, PLANES_S + planes + shift
        else:
            from_x, to_x, count = PLANES_S, PLANES_S, planes
        from_y, count_y, to_y = part(dy, rows, ROWS)
        return (
            src.at[pl.ds(from_x, count), pl.ds(ROWS + from_y, count_y)],
            src.at[pl.ds(to_x, count), pl.ds(to_y, count_y)],
            dx,
            dy,
        )

    near_copies = copies_of(1, [source_piece(dx, dy, 0, near) for dx, dy in WAYS])
    own_pressure.wait()
    finished(pressure_copies)
    finished(near_copies)

    sweep(pa, pb, src, 4, planes + 8, -1, 1.0)
    sweep(pb, pa, src, 5, planes + 7, -1, 1.0)

    def restrict0(m):
        fine0[m] = leftover(pa, src, 2 * m + 6, -1, 1.0, rows) + leftover(
            pa, src, 2 * m + 7, -1, 1.0, rows
        )

    loop(0, planes1, restrict0, 2)
    half0[...] = spread(
        fine0[...].reshape(planes1 * rows, depth), down_z0[...]
    ).reshape(planes1, rows, depth1)
    for m in range(planes1):
        r1[m + PLANES_1, pl.ds(ROWS, rows1), :] = 0.125 * (
            half0[m, pl.ds(0, rows1, stride=2), :] + half0[m, pl.ds(1, rows1, stride=2), :]
        )

    def residual_piece(dx, dy):
        from_x, count_x, to_x = part(dx, planes1, PLANES_1)
        from_y, count_y, to_y = part(dy, rows1, ROWS)
        return (
            r1.at[pl.ds(PLANES_1 + from_x, count_x), pl.ds(ROWS + from_y, count_y)],
            r1.at[pl.ds(to_x, count_x), pl.ds(to_y, count_y)],
            dx,
            dy,
        )

    coarse_copies = copies_of(3, [residual_piece(dx, dy) for dx, dy in WAYS])

    sideways = [(dx, dy) for dx, dy in WAYS if dx]
    far_copies = copies_of(2, [source_piece(dx, dy, near, far) for dx, dy in sideways])
    far_copies += copies_of(
        9,
        [
            pressure_piece(dx, dy, near_pressure, PLANES_P - near_pressure)
            for dx, dy in sideways
        ],
    )
    finished(coarse_copies)

    p1a[...] = (-4.0 * weight) * r1[...]
    sweep(p1a, p1b, r1, 1, planes1 + 9, 0, 4.0)

    def restrict1(m):
        fine1[m] = leftover(p1b, r1, 2 * m + 3, 0, 4.0, rows1) + leftover(
            p1b, r1, 2 * m + 4, 0, 4.0, rows1
        )

    loop(0, planes2 + 2, restrict1, 2)
    half1[...] = spread(
        fine1[...].reshape((planes2 + 2) * rows1, depth1), down_z1[...]
    ).reshape(planes2 + 2, rows1, depth1)
    for m in range(planes2 + 2):
        value = 0.125 * (
            half1[m, pl.ds(0, rows2, stride=2), :] + half1[m, pl.ds(1, rows2, stride=2), :]
        )
        r2s[m] = value
        if 0 < m <= planes2:
            r2[m + PLANES_2 - 1, pl.ds(ROWS, rows2), :] = value

    def coarsest_piece(dx, dy):
        from_x, count_x, to_x = {
            1: (0, PLANES_2, 0),
            -1: (1, PLANES_2, PLANES_2 + planes2),
            0: (1, planes2, PLANES_2),
        }[dx]
        from_y, count_y, to_y = part(dy, rows2, ROWS)
        return (
            r2s.at[pl.ds(from_x, count_x), pl.ds(from_y, count_y)],
            r2.at[pl.ds(to_x, count_x), pl.ds(to_y, count_y)],
            dx,
            dy,
        )

    coarsest_copies = copies_of(4, [coarsest_piece(dx, dy) for dx, dy in WAYS])

    finished(far_copies)
    sweep(pa, pb, src, 1, 4, -1, 1.0)
    sweep(pa, pb, src, planes + 8, planes + 11, -1, 1.0)
    sweep(pb, pa, src, 2, 5, -1, 1.0)
    sweep(pb, pa, src, planes + 7, planes + 10, -1, 1.0)
    finished(coarsest_copies)

    c2a[...] = (-16.0 * weight) * r2[...]
    sweep(c2a, c2b, r2, 1, planes2 + 9, 0, 16.0)
    sweep(c2b, c2a, r2, 2, planes2 + 8, 0, 16.0)
    sweep(c2a, c2b, r2, 3, planes2 + 7, 0, 16.0)

    def prolong(coarse, count, tall, wide, table):
        half = tall.shape[1] // 2
        for m in range(count):
            value = coarse[m + 3, pl.ds(ROWS // 2, half), :]
            tall[m, pl.ds(0, half, stride=2), :] = value
            tall[m, pl.ds(1, half, stride=2), :] = value
        wide[...] = spread(
            tall[...].reshape(count * tall.shape[1], tall.shape[2]), table[...]
        ).reshape(wide.shape)

    def add_pair(fine, wide, m, first):
        value = wide[m]
        fine[first] = fine[first] + value
        fine[first + 1] = fine[first + 1] + value

    prolong(c2b, planes2 + 4, tall1, rise1, up_z1)
    loop(0, planes2 + 4, lambda m: add_pair(p1b, rise1, m, 2 * m + 1))
    sweep(p1b, p1a, r1, 2, planes1 + 8, 0, 4.0)
    sweep(p1a, p1b, r1, 3, planes1 + 7, 0, 4.0)

    prolong(p1b, planes1 + 4, tall0, rise0, up_z0)
    loop(0, planes1 + 4, lambda m: add_pair(pa, rise0, m, 2 * m + 2))
    sweep(pa, pb, src, 3, planes + 9, -1, 1.0)

    def last(i):
        total, mid = own_rows(pb, i, rows)
        total = total - src[i - 1, pl.ds(ROWS, rows), :]
        pa[i, pl.ds(ROWS, rows), :] = (1.0 - relax_weight) * mid + weight * total

    loop(4, planes + 8, last)

    tile = pl.ds(ROWS, rows)
    potential_copy = here(pa.at[pl.ds(PLANES_P, planes), tile], potential_out, 0)

    def own_planes(index):
        return pl.ds(PLANES_P + index * thick, thick)

    back_at = out.at[0, :, mine, :]
    back = []
    for ahead in range(1, members):
        device = member(sizes, ahead)
        back.append(
            copy_to(10, ahead - 1, pa.at[own_planes(device[1]), tile], back_at, device)
        )
    own_back = here(pa.at[own_planes(me_y), tile], back_at, 1)

    def slope_of(k):
        ahead = pa[k + 7, tile, :] - pa[k + 5, tile, :]
        further = pa[k + 8, tile, :] - pa[k + 4, tile, :]
        leaf[k] = (8.0 * ahead - further) * (1.0 / 12.0)

    slope_at = out.at[1, :, mine, :]
    for ahead in range(1, members + 1):
        device = member(sizes, ahead)
        for p in range(thick):
            slope_of(device[1] * thick + p)
        source = leaf.at[pl.ds(device[1] * thick, thick)]
        if ahead < members:
            back.append(copy_to(11, ahead - 1, source, slope_at, device))
        else:
            own_slope = here(source, slope_at, 2)
    potential_copy.wait()
    own_back.wait()
    own_slope.wait()
    finished(back)
    star_copy.wait()


def pairing(fine, coarse, wrap=0):
    coarse_at = np.arange(coarse)
    if wrap:
        coarse_at = coarse_at % wrap
    return (np.arange(fine)[:, None] // 2 == coarse_at[None, :]).astype(np.float32)


def two_parts(table):
    upper = table.astype(ml_dtypes.bfloat16)
    lower = (table - upper.astype(np.float32)).astype(ml_dtypes.bfloat16)
    return [jnp.asarray(upper), jnp.asarray(lower)]


def predict_and_cycle(velocity, obstacle, pressure, row_tables, depth_tables, sizes):
    planes, rows, depth = pressure.shape
    _, thick, height, _ = velocity.shape
    planes1, rows1, depth1 = planes // 2, rows // 2, depth // 2
    planes2, rows2, depth2 = planes // 4, rows // 4, depth // 4
    down_z0 = pairing(depth, depth1)
    down_z1 = pairing(depth1, depth1, depth2)
    up_z1 = pairing(depth1, depth1).T
    up_z0 = pairing(depth, depth1).T
    tables = two_parts(np.concatenate(row_tables, axis=0))
    tables += two_parts(np.concatenate([table.T for table in depth_tables], axis=1))
    before, after = stream_planes(velocity)
    across = transverse(velocity, tables)
    tables += [
        jnp.asarray(table, jnp.bfloat16) for table in (down_z0, down_z1, up_z1, up_z0)
    ]

    def vmem(*shape):
        return pltpu.VMEM(shape, jnp.float32)

    return pl.pallas_call(
        functools.partial(cycle_kernel, sizes),
        out_shape=(
            jax.ShapeDtypeStruct(velocity.shape, jnp.float32),
            jax.ShapeDtypeStruct(pressure.shape, jnp.float32),
            jax.ShapeDtypeStruct((2, thick, height, depth), jnp.float32),
        ),
        in_specs=[pl.BlockSpec(memory_space=pl.ANY)] * 6
        + [pl.BlockSpec(memory_space=pltpu.VMEM)] * len(tables),
        out_specs=(
            pl.BlockSpec(memory_space=pl.ANY),
            pl.BlockSpec(memory_space=pl.ANY),
            pl.BlockSpec(memory_space=pltpu.VMEM),
        ),
        scratch_shapes=[
            vmem(3, thick, height, depth),
            vmem(planes, rows, depth),
            pltpu.VMEM((thick, height, depth), jnp.int32),
            vmem(3, thick, height, depth),
            vmem(3, thick, height, depth),
            vmem(3, thick, height, depth),
            vmem(3, thick, height, depth),
            vmem(thick, height, depth),
            pltpu.VMEM((height, depth), jnp.bfloat16),
            pltpu.VMEM((height, depth), jnp.bfloat16),
            vmem(planes + 12, rows + 16, depth),
            vmem(planes + 12, rows + 16, depth),
            vmem(planes + 10, rows + 16, depth),
            vmem(planes + 4, rows, depth),
            vmem(planes1, rows, depth),
            vmem(planes1, rows, depth1),
            vmem(planes1 + 10, rows1 + 16, depth1),
            vmem(planes1 + 10, rows1 + 16, depth1),
            vmem(planes1 + 10, rows1 + 16, depth1),
            vmem(planes2 + 2, rows1, depth1),
            vmem(planes2 + 2, rows1, depth1),
            vmem(planes2 + 2, rows2, depth1),
            vmem(planes2 + 10, rows2 + 16, depth1),
            vmem(planes2 + 10, rows2 + 16, depth1),
            vmem(planes2 + 10, rows2 + 16, depth1),
            vmem(planes2 + 4, rows1 + 16, depth1),
            vmem(planes2 + 4, rows1 + 16, depth1),
            vmem(planes1 + 4, rows + 16, depth1),
            vmem(planes1 + 4, rows + 16, depth),
            pltpu.SemaphoreType.DMA((18,)),
            pltpu.SemaphoreType.DMA((12, 8)),
            pltpu.SemaphoreType.DMA((12, 8)),
        ],
        compiler_params=pltpu.CompilerParams(
            collective_id=1, has_side_effects=True, vmem_limit_bytes=40 * 2**20
        ),
        name="predict_and_cycle",
    )(velocity, before, after, across, obstacle, pressure, *tables)


def local(sizes, velocity, obstacle, pressure):
    row_tables = compact_tables(velocity.shape[2])
    depth_tables = compact_tables(velocity.shape[3])
    keep = 1.0 - obstacle.astype(jnp.float32)
    star, potential, returned = predict_and_cycle(
        velocity, obstacle, pressure, row_tables, depth_tables, sizes
    )
    gradient = jnp.stack(
        [
            returned[1],
            along_rows(row_tables[0], returned[0]),
            along_depth(depth_tables[0], returned[0]),
        ]
    )
    corrected = (star - gradient) * keep
    return (corrected, potential)


def solution(mesh):
    in_specs = (
        P(None, ("tunnel", "group"), None, None),
        P(("tunnel", "group"), None, None),
        P("tunnel", "group", None),
    )
    out_specs = (P(None, ("tunnel", "group"), None, None), P("tunnel", "group", None))
    sizes = (mesh.shape["tunnel"], mesh.shape["group"])
    return jax.shard_map(
        functools.partial(local, sizes),
        mesh=mesh,
        in_specs=in_specs,
        out_specs=out_specs,
        check_vma=False,
    )
```

```python
import functools
import math

import jax
import jax.numpy as jnp
import ml_dtypes
import numpy as np
from jax import lax
from jax.experimental import pallas as pl
from jax.experimental.pallas import tpu as pltpu
from jax.sharding import PartitionSpec as P

time_step = 0.1
viscosity = 0.05
relax_weight = 0.8
high = lax.Precision.HIGH
MESH = pl.DeviceIdType.MESH

ROWS = 8
PLANES_P = 6
PLANES_S = 5
PLANES_1 = 5
PLANES_2 = 5
WAYS = [(dx, dy) for dx in (-1, 0, 1) for dy in (-1, 0, 1) if (dx, dy) != (0, 0)]


def compact_tables(count):
    indices = np.arange(count)
    angles = (indices[:, None] * indices[None, :] % count) * (2.0 * math.pi / count)
    cosines = np.cos(angles)
    sines = np.sin(angles)
    theta = indices * (2.0 * math.pi / count)
    first_wave = (14.0 / 9.0 * np.sin(theta) + np.sin(2.0 * theta) / 18.0) / (
        1.0 + 2.0 / 3.0 * np.cos(theta)
    )
    second_wave = (
        24.0 / 11.0 * (1.0 - np.cos(theta)) + 3.0 / 22.0 * (1.0 - np.cos(2.0 * theta))
    ) / (1.0 + 4.0 / 11.0 * np.cos(theta))
    first = ((cosines * first_wave) @ sines.T - (sines * first_wave) @ cosines.T) / count
    second = -((cosines * second_wave) @ cosines.T + (sines * second_wave) @ sines.T) / count
    return first.astype(np.float32), second.astype(np.float32)


def along_rows(matrix, field):
    return jnp.einsum("ij,...jz->...iz", matrix, field, precision=high)


def along_depth(matrix, field):
    return jnp.einsum("...j,ij->...i", field, matrix, precision=high)


def part(step, length, halo):
    if step > 0:
        return length - halo, halo, 0
    if step < 0:
        return 0, halo, halo + length
    return 0, length, halo


def neighbour(sizes, dx, dy):
    me_x = lax.axis_index("tunnel")
    me_y = lax.axis_index("group")
    return (
        lax.rem(me_x + (dx + sizes[0]), sizes[0]),
        lax.rem(me_y + (dy + sizes[1]), sizes[1]),
    )


def stream_planes(value):
    size = lax.axis_size(("tunnel", "group"))
    up = [(i, (i + 1) % size) for i in range(size)]
    down = [(j, i) for i, j in up]
    before = lax.ppermute(value, ("tunnel", "group"), up)
    after = lax.ppermute(value, ("tunnel", "group"), down)
    return before, after


def member(sizes, ahead):
    return lax.axis_index("tunnel"), lax.rem(lax.axis_index("group") + ahead, sizes[1])


def enter(sizes):
    barrier = pltpu.get_barrier_semaphore()
    partners = [neighbour(sizes, dx, dy) for dx, dy in WAYS]
    partners += [member(sizes, ahead) for ahead in range(1, sizes[1])]
    for partner in partners:
        pl.semaphore_signal(barrier, inc=1, device_id=partner, device_id_type=MESH)
    pl.semaphore_wait(barrier, len(partners))


def loop(start, stop, body, unroll=4):
    whole = (stop - start) // unroll

    def several(step, carry):
        for lane in range(unroll):
            body(start + step * unroll + lane)
        return carry

    if whole:
        lax.fori_loop(0, whole, several, 0)
    for index in range(start + whole * unroll, stop):
        body(index)


def around(value):
    rows, depth = value.shape
    total = pltpu.roll(value, 1, 0) + pltpu.roll(value, rows - 1, 0)
    return total + pltpu.roll(value, 1, 1) + pltpu.roll(value, depth - 1, 1)


def sweep(source, target, right, start, stop, offset, scale):
    weight = relax_weight / 6.0

    def body(i):
        mid = source[i]
        total = source[i + 1] + source[i - 1] + around(mid)
        if scale == 1.0:
            total = total - right[i + offset]
        else:
            total = total - scale * right[i + offset]
        target[i] = (1.0 - relax_weight) * mid + weight * total

    loop(start, stop, body)


def own_rows(source, i, rows):
    span = source[i]
    rolled = pltpu.roll(span, 1, 0) + pltpu.roll(span, rows + 2 * ROWS - 1, 0)
    inside = pl.ds(ROWS, rows)
    mid = source[i, inside, :]
    total = source[i + 1, inside, :] + source[i - 1, inside, :] + rolled[ROWS : ROWS + rows]
    depth = mid.shape[1]
    return total + pltpu.roll(mid, 1, 1) + pltpu.roll(mid, depth - 1, 1), mid


def leftover(source, right, i, offset, scale, rows):
    total, mid = own_rows(source, i, rows)
    return right[i + offset, pl.ds(ROWS, rows), :] - (total - 6.0 * mid) * (1.0 / scale)


def spread(value, table):
    upper = value.astype(jnp.bfloat16)
    lower = (value - upper.astype(jnp.float32)).astype(jnp.bfloat16)
    return jnp.dot(upper, table, preferred_element_type=jnp.float32) + jnp.dot(
        lower, table, preferred_element_type=jnp.float32
    )


def halves(value):
    upper = value.astype(jnp.bfloat16)
    return upper, (value - upper.astype(jnp.float32)).astype(jnp.bfloat16)


def product(a, b):
    return jnp.dot(a, b, preferred_element_type=jnp.float32)


def transverse_kernel(vel, rows_high, rows_low, depth_high, depth_low, base, high, low):
    height, depth = vel.shape[2], vel.shape[3]
    first, second = pl.ds(0, height), pl.ds(height, height)

    def component(c, carry):
        upper, lower = halves(vel[c, 0])
        high[...] = upper
        low[...] = lower
        row_first = (
            product(rows_high[first, :], high[...])
            + product(rows_high[first, :], low[...])
            + product(rows_low[first, :], high[...])
        )
        row_second = (
            product(rows_high[second, :], high[...])
            + product(rows_high[second, :], low[...])
            + product(rows_low[second, :], high[...])
        )
        along = (
            product(high[...], depth_high[...])
            + product(low[...], depth_high[...])
            + product(high[...], depth_low[...])
        )
        advection = vel[1, 0] * row_first + vel[2, 0] * along[:, :depth]
        base[c, 0] = vel[c, 0] + time_step * (
            viscosity * (row_second + along[:, depth:]) - advection
        )
        return carry

    lax.fori_loop(0, 3, component, 0)


def transverse(velocity, tables):
    _, thick, height, depth = velocity.shape
    plane = pl.BlockSpec((3, 1, height, depth), lambda p: (0, p, 0, 0))
    flops = 2 * 9 * thick * height * depth * 2 * (height + depth)
    return pl.pallas_call(
        transverse_kernel,
        grid=(thick,),
        out_shape=jax.ShapeDtypeStruct(velocity.shape, jnp.float32),
        in_specs=[plane] + [pl.BlockSpec(memory_space=pltpu.VMEM)] * 4,
        out_specs=plane,
        scratch_shapes=[pltpu.VMEM((height, depth), jnp.bfloat16)] * 2,
        compiler_params=pltpu.CompilerParams(vmem_limit_bytes=32 * 2**20),
        cost_estimate=pl.CostEstimate(
            flops=flops, bytes_accessed=8 * 3 * thick * height * depth, transcendentals=0
        ),
        name="transverse",
    )(velocity, *tables)


def cycle_kernel(
    sizes,
    velocity,
    before,
    after,
    across,
    obstacle,
    pressure,
    rows_high,
    rows_low,
    depth_high,
    depth_low,
    down_z0,
    down_z1,
    up_z1,
    up_z0,
    star_out,
    potential_out,
    out,
    vel,
    leaf,
    solid,
    left,
    right,
    base,
    stars,
    cross,
    high,
    low,
    pa,
    pb,
    src,
    star,
    fine0,
    half0,
    r1,
    p1a,
    p1b,
    fine1,
    half1,
    r2s,
    r2,
    c2a,
    c2b,
    tall1,
    rise1,
    tall0,
    rise0,
    local_sem,
    send_sem,
    recv_sem,
):
    planes, rows, depth = pressure.shape
    planes1, rows1, depth1 = planes // 2, rows // 2, depth // 2
    planes2, rows2 = planes // 4, rows // 4
    weight = relax_weight / 6.0
    near, far = 2, PLANES_S - 2
    thick, height = velocity.shape[1], velocity.shape[2]
    members = sizes[1]
    me_y = lax.axis_index("group")

    def copy_to(group, way, source, target, device):
        copy = pltpu.make_async_remote_copy(
            src_ref=source,
            dst_ref=target,
            send_sem=send_sem.at[group, way],
            recv_sem=recv_sem.at[group, way],
            device_id=device,
            device_id_type=MESH,
        )
        copy.start()
        return copy

    def copies_of(group, pieces):
        return [
            copy_to(group, way, source, target, neighbour(sizes, dx, dy))
            for way, (source, target, dx, dy) in enumerate(pieces)
        ]

    def finished(copies):
        for copy in copies:
            copy.wait()

    def here(source, target, index):
        copy = pltpu.make_async_copy(source, target, local_sem.at[index])
        copy.start()
        return copy

    def load(c):
        pairs = [(velocity, vel), (before, left), (after, right), (across, base)]
        return [
            here(source.at[c], target.at[c], 6 + 4 * c + index)
            for index, (source, target) in enumerate(pairs)
        ]

    loads = [load(0)]
    own_solid = here(obstacle, solid, 1)
    loads += [load(1), load(2)]
    own_pressure = here(pressure, pa.at[pl.ds(PLANES_P, planes), pl.ds(ROWS, rows)], 2)
    enter(sizes)

    near_pressure = PLANES_P // 2

    def pressure_piece(dx, dy, shift, count):
        if dx > 0:
            from_x, to_x = planes - shift - count, PLANES_P - shift - count
        elif dx < 0:
            from_x, to_x = shift, PLANES_P + planes + shift
        else:
            from_x, to_x, count = 0, PLANES_P, planes
        from_y, count_y, to_y = part(dy, rows, ROWS)
        return (
            pressure.at[pl.ds(from_x, count), pl.ds(from_y, count_y)],
            pa.at[pl.ds(to_x, count), pl.ds(to_y, count_y)],
            dx,
            dy,
        )

    pressure_copies = copies_of(
        5, [pressure_piece(dx, dy, 0, near_pressure) for dx, dy in WAYS]
    )

    def block(index):
        return pl.ds(pl.multiple_of(index * rows, rows), rows)

    def predict(c, at):
        near_planes = [left.at[c, 0], left.at[c, 1], vel.at[c, 0], vel.at[c, 1]]
        near_planes += [right.at[c, 0], right.at[c, 1]]
        f = [plane[at, :] for plane in near_planes]
        for p in range(thick):
            ahead, further = f[p + 3] - f[p + 1], f[p + 4] - f[p]
            slope = (8.0 * ahead - further) * (1.0 / 12.0)
            beside, beyond = f[p + 3] + f[p + 1], f[p + 4] + f[p]
            bend = (16.0 * beside - beyond - 30.0 * f[p + 2]) * (1.0 / 12.0)
            keep = 1.0 - solid[p, at, :].astype(jnp.float32)
            stars[c, p, at, :] = keep * (
                base[c, p, at, :]
                + time_step * (viscosity * bend - vel[0, p, at, :] * slope)
            )

    def slabs(group, make, source, target):
        copies = []
        for ahead in range(1, members):
            device = member(sizes, ahead)
            at = block(device[1])
            make(at)
            copies.append(copy_to(group, ahead - 1, source(at), target, device))
        make(block(me_y))
        return copies

    mine = block(me_y)

    finished(loads[0])
    own_solid.wait()
    star_at = star.at[pl.ds(2 + me_y * thick, thick)]
    star_slabs = slabs(
        7, lambda at: predict(0, at), lambda at: stars.at[0, :, at, :], star_at
    )
    own_star = here(stars.at[0, :, mine, :], star_at, 3)

    finished(loads[1])
    loop(0, members, lambda k: predict(1, block(k)), 2)
    for p in range(thick):
        upper, lower = halves(stars[1, p])
        high[...] = upper
        low[...] = lower
        first = pl.ds(0, height)
        cross[p] = (
            product(rows_high[first, :], high[...])
            + product(rows_high[first, :], low[...])
            + product(rows_low[first, :], high[...])
        )

    finished(loads[2])

    def diverge(at):
        predict(2, at)
        wave_high, wave_low = depth_high[:, pl.ds(0, depth)], depth_low[:, pl.ds(0, depth)]
        upper, lower = halves(stars[2, :, at, :].reshape(thick * rows, depth))
        along = product(upper, wave_high) + product(lower, wave_high) + product(upper, wave_low)
        for p in range(thick):
            cross[p, at, :] = cross[p, at, :] + along[p * rows : (p + 1) * rows]

    src_at = src.at[pl.ds(PLANES_S + me_y * thick, thick), pl.ds(ROWS, rows)]
    src_slabs = slabs(8, diverge, lambda at: cross.at[:, at, :], src_at)
    own_src = here(cross.at[:, mine, :], src_at, 4)
    star_copy = here(stars, star_out, 5)
    own_star.wait()
    finished(star_slabs)
    star_copies = copies_of(
        0,
        [
            (star.at[pl.ds(planes, 2)], star.at[pl.ds(0, 2)], 1, 0),
            (star.at[pl.ds(2, 2)], star.at[pl.ds(planes + 2, 2)], -1, 0),
        ],
    )

    finished(star_copies)
    own_src.wait()
    finished(src_slabs)

    def divergence(k):
        inside = pl.ds(ROWS, rows)
        ahead = star[k + 3] - star[k + 1]
        further = star[k + 4] - star[k]
        src[k + PLANES_S, inside, :] = src[k + PLANES_S, inside, :] + (
            8.0 * ahead - further
        ) * (1.0 / 12.0)

    loop(0, planes, divergence)

    def source_piece(dx, dy, shift, count):
        if dx > 0:
            from_x, to_x = PLANES_S + planes - shift - count, PLANES_S - shift - count
        elif dx < 0:
            from_x, to_x = PLANES_S + shift, PLANES_S + planes + shift
        else:
            from_x, to_x, count = PLANES_S, PLANES_S, planes
        from_y, count_y, to_y = part(dy, rows, ROWS)
        return (
            src.at[pl.ds(from_x, count), pl.ds(ROWS + from_y, count_y)],
            src.at[pl.ds(to_x, count), pl.ds(to_y, count_y)],
            dx,
            dy,
        )

    near_copies = copies_of(1, [source_piece(dx, dy, 0, near) for dx, dy in WAYS])
    own_pressure.wait()
    finished(pressure_copies)
    finished(near_copies)

    sweep(pa, pb, src, 4, planes + 8, -1, 1.0)
    sweep(pb, pa, src, 5, planes + 7, -1, 1.0)

    def restrict0(m):
        fine0[m] = leftover(pa, src, 2 * m + 6, -1, 1.0, rows) + leftover(
            pa, src, 2 * m + 7, -1, 1.0, rows
        )

    loop(0, planes1, restrict0, 2)
    half0[...] = spread(
        fine0[...].reshape(planes1 * rows, depth), down_z0[...]
    ).reshape(planes1, rows, depth1)
    for m in range(planes1):
        r1[m + PLANES_1, pl.ds(ROWS, rows1), :] = 0.125 * (
            half0[m, pl.ds(0, rows1, stride=2), :] + half0[m, pl.ds(1, rows1, stride=2), :]
        )

    def residual_piece(dx, dy):
        from_x, count_x, to_x = part(dx, planes1, PLANES_1)
        from_y, count_y, to_y = part(dy, rows1, ROWS)
        return (
            r1.at[pl.ds(PLANES_1 + from_x, count_x), pl.ds(ROWS + from_y, count_y)],
            r1.at[pl.ds(to_x, count_x), pl.ds(to_y, count_y)],
            dx,
            dy,
        )

    coarse_copies = copies_of(3, [residual_piece(dx, dy) for dx, dy in WAYS])

    sideways = [(dx, dy) for dx, dy in WAYS if dx]
    far_copies = copies_of(2, [source_piece(dx, dy, near, far) for dx, dy in sideways])
    far_copies += copies_of(
        9,
        [
            pressure_piece(dx, dy, near_pressure, PLANES_P - near_pressure)
            for dx, dy in sideways
        ],
    )
    finished(coarse_copies)

    p1a[...] = (-4.0 * weight) * r1[...]
    sweep(p1a, p1b, r1, 1, planes1 + 9, 0, 4.0)

    def restrict1(m):
        fine1[m] = leftover(p1b, r1, 2 * m + 3, 0, 4.0, rows1) + leftover(
            p1b, r1, 2 * m + 4, 0, 4.0, rows1
        )

    loop(0, planes2 + 2, restrict1, 2)
    half1[...] = spread(
        fine1[...].reshape((planes2 + 2) * rows1, depth1), down_z1[...]
    ).reshape(planes2 + 2, rows1, depth1)
    for m in range(planes2 + 2):
        value = 0.125 * (
            half1[m, pl.ds(0, rows2, stride=2), :] + half1[m, pl.ds(1, rows2, stride=2), :]
        )
        r2s[m] = value
        if 0 < m <= planes2:
            r2[m + PLANES_2 - 1, pl.ds(ROWS, rows2), :] = value

    def coarsest_piece(dx, dy):
        from_x, count_x, to_x = {
            1: (0, PLANES_2, 0),
            -1: (1, PLANES_2, PLANES_2 + planes2),
            0: (1, planes2, PLANES_2),
        }[dx]
        from_y, count_y, to_y = part(dy, rows2, ROWS)
        return (
            r2s.at[pl.ds(from_x, count_x), pl.ds(from_y, count_y)],
            r2.at[pl.ds(to_x, count_x), pl.ds(to_y, count_y)],
            dx,
            dy,
        )

    coarsest_copies = copies_of(4, [coarsest_piece(dx, dy) for dx, dy in WAYS])

    finished(far_copies)
    sweep(pa, pb, src, 1, 4, -1, 1.0)
    sweep(pa, pb, src, planes + 8, planes + 11, -1, 1.0)
    sweep(pb, pa, src, 2, 5, -1, 1.0)
    sweep(pb, pa, src, planes + 7, planes + 10, -1, 1.0)
    finished(coarsest_copies)

    c2a[...] = (-16.0 * weight) * r2[...]
    sweep(c2a, c2b, r2, 1, planes2 + 9, 0, 16.0)
    sweep(c2b, c2a, r2, 2, planes2 + 8, 0, 16.0)
    sweep(c2a, c2b, r2, 3, planes2 + 7, 0, 16.0)

    def prolong(coarse, count, tall, wide, table):
        half = tall.shape[1] // 2
        for m in range(count):
            value = coarse[m + 3, pl.ds(ROWS // 2, half), :]
            tall[m, pl.ds(0, half, stride=2), :] = value
            tall[m, pl.ds(1, half, stride=2), :] = value
        wide[...] = spread(
            tall[...].reshape(count * tall.shape[1], tall.shape[2]), table[...]
        ).reshape(wide.shape)

    def add_pair(fine, wide, m, first):
        value = wide[m]
        fine[first] = fine[first] + value
        fine[first + 1] = fine[first + 1] + value

    prolong(c2b, planes2 + 4, tall1, rise1, up_z1)
    loop(0, planes2 + 4, lambda m: add_pair(p1b, rise1, m, 2 * m + 1))
    sweep(p1b, p1a, r1, 2, planes1 + 8, 0, 4.0)
    sweep(p1a, p1b, r1, 3, planes1 + 7, 0, 4.0)

    prolong(p1b, planes1 + 4, tall0, rise0, up_z0)
    loop(0, planes1 + 4, lambda m: add_pair(pa, rise0, m, 2 * m + 2))
    sweep(pa, pb, src, 3, planes + 9, -1, 1.0)

    def last(i):
        total, mid = own_rows(pb, i, rows)
        total = total - src[i - 1, pl.ds(ROWS, rows), :]
        pa[i, pl.ds(ROWS, rows), :] = (1.0 - relax_weight) * mid + weight * total

    loop(4, planes + 8, last)

    tile = pl.ds(ROWS, rows)
    potential_copy = here(pa.at[pl.ds(PLANES_P, planes), tile], potential_out, 0)

    def own_planes(index):
        return pl.ds(PLANES_P + index * thick, thick)

    back_at = out.at[0, :, mine, :]
    back = []
    for ahead in range(1, members):
        device = member(sizes, ahead)
        back.append(
            copy_to(10, ahead - 1, pa.at[own_planes(device[1]), tile], back_at, device)
        )
    own_back = here(pa.at[own_planes(me_y), tile], back_at, 1)

    def slope_of(k):
        ahead = pa[k + 7, tile, :] - pa[k + 5, tile, :]
        further = pa[k + 8, tile, :] - pa[k + 4, tile, :]
        leaf[k] = (8.0 * ahead - further) * (1.0 / 12.0)

    slope_at = out.at[1, :, mine, :]
    for ahead in range(1, members + 1):
        device = member(sizes, ahead)
        for p in range(thick):
            slope_of(device[1] * thick + p)
        source = leaf.at[pl.ds(device[1] * thick, thick)]
        if ahead < members:
            back.append(copy_to(11, ahead - 1, source, slope_at, device))
        else:
            own_slope = here(source, slope_at, 2)
    potential_copy.wait()
    own_back.wait()
    own_slope.wait()
    finished(back)
    star_copy.wait()


def pairing(fine, coarse, wrap=0):
    coarse_at = np.arange(coarse)
    if wrap:
        coarse_at = coarse_at % wrap
    return (np.arange(fine)[:, None] // 2 == coarse_at[None, :]).astype(np.float32)


def two_parts(table):
    upper = table.astype(ml_dtypes.bfloat16)
    lower = (table - upper.astype(np.float32)).astype(ml_dtypes.bfloat16)
    return [jnp.asarray(upper), jnp.asarray(lower)]


def predict_and_cycle(velocity, obstacle, pressure, row_tables, depth_tables, sizes):
    planes, rows, depth = pressure.shape
    _, thick, height, _ = velocity.shape
    planes1, rows1, depth1 = planes // 2, rows // 2, depth // 2
    planes2, rows2, depth2 = planes // 4, rows // 4, depth // 4
    down_z0 = pairing(depth, depth1)
    down_z1 = pairing(depth1, depth1, depth2)
    up_z1 = pairing(depth1, depth1).T
    up_z0 = pairing(depth, depth1).T
    tables = two_parts(np.concatenate(row_tables, axis=0))
    tables += two_parts(np.concatenate([table.T for table in depth_tables], axis=1))
    before, after = stream_planes(velocity)
    across = transverse(velocity, tables)
    tables += [
        jnp.asarray(table, jnp.bfloat16) for table in (down_z0, down_z1, up_z1, up_z0)
    ]

    def vmem(*shape):
        return pltpu.VMEM(shape, jnp.float32)

    return pl.pallas_call(
        functools.partial(cycle_kernel, sizes),
        out_shape=(
            jax.ShapeDtypeStruct(velocity.shape, jnp.float32),
            jax.ShapeDtypeStruct(pressure.shape, jnp.float32),
            jax.ShapeDtypeStruct((2, thick, height, depth), jnp.float32),
        ),
        in_specs=[pl.BlockSpec(memory_space=pl.ANY)] * 6
        + [pl.BlockSpec(memory_space=pltpu.VMEM)] * len(tables),
        out_specs=(
            pl.BlockSpec(memory_space=pl.ANY),
            pl.BlockSpec(memory_space=pl.ANY),
            pl.BlockSpec(memory_space=pltpu.VMEM),
        ),
        scratch_shapes=[
            vmem(3, thick, height, depth),
            vmem(planes, rows, depth),
            pltpu.VMEM((thick, height, depth), jnp.int32),
            vmem(3, thick, height, depth),
            vmem(3, thick, height, depth),
            vmem(3, thick, height, depth),
            vmem(3, thick, height, depth),
            vmem(thick, height, depth),
            pltpu.VMEM((height, depth), jnp.bfloat16),
            pltpu.VMEM((height, depth), jnp.bfloat16),
            vmem(planes + 12, rows + 16, depth),
            vmem(planes + 12, rows + 16, depth),
            vmem(planes + 10, rows + 16, depth),
            vmem(planes + 4, rows, depth),
            vmem(planes1, rows, depth),
            vmem(planes1, rows, depth1),
            vmem(planes1 + 10, rows1 + 16, depth1),
            vmem(planes1 + 10, rows1 + 16, depth1),
            vmem(planes1 + 10, rows1 + 16, depth1),
            vmem(planes2 + 2, rows1, depth1),
            vmem(planes2 + 2, rows1, depth1),
            vmem(planes2 + 2, rows2, depth1),
            vmem(planes2 + 10, rows2 + 16, depth1),
            vmem(planes2 + 10, rows2 + 16, depth1),
            vmem(planes2 + 10, rows2 + 16, depth1),
            vmem(planes2 + 4, rows1 + 16, depth1),
            vmem(planes2 + 4, rows1 + 16, depth1),
            vmem(planes1 + 4, rows + 16, depth1),
            vmem(planes1 + 4, rows + 16, depth),
            pltpu.SemaphoreType.DMA((18,)),
            pltpu.SemaphoreType.DMA((12, 8)),
            pltpu.SemaphoreType.DMA((12, 8)),
        ],
        compiler_params=pltpu.CompilerParams(
            collective_id=1, has_side_effects=True, vmem_limit_bytes=37 * 2**20
        ),
        name="predict_and_cycle",
    )(velocity, before, after, across, obstacle, pressure, *tables)


def local(sizes, velocity, obstacle, pressure):
    row_tables = compact_tables(velocity.shape[2])
    depth_tables = compact_tables(velocity.shape[3])
    keep = 1.0 - obstacle.astype(jnp.float32)
    star, potential, returned = predict_and_cycle(
        velocity, obstacle, pressure, row_tables, depth_tables, sizes
    )
    gradient = jnp.stack(
        [
            returned[1],
            along_rows(row_tables[0], returned[0]),
            along_depth(depth_tables[0], returned[0]),
        ]
    )
    corrected = (star - gradient) * keep
    return (corrected, potential)


def solution(mesh):
    in_specs = (
        P(None, ("tunnel", "group"), None, None),
        P(("tunnel", "group"), None, None),
        P("tunnel", "group", None),
    )
    out_specs = (P(None, ("tunnel", "group"), None, None), P("tunnel", "group", None))
    sizes = (mesh.shape["tunnel"], mesh.shape["group"])
    return jax.shard_map(
        functools.partial(local, sizes),
        mesh=mesh,
        in_specs=in_specs,
        out_specs=out_specs,
        check_vma=False,
    )
```
